32 devices in a mesh: shape: 4 (over z), grp: 8 (over y, x, core).
Axes of the slice: x: 2, y: 2, z: 4, core: 2. Of those that a mesh axis runs over, the one named last changes fastest.
Arguments:
- latents: bfloat16 [128, 64, 64, 128], P(('shape', 'grp')), parts along dimension 0, may hold values from -6 to 6
- up_weight: bfloat16 [3, 3, 3, 128, 64], replicated, may hold values from -0.25 to 0.25
- first_weight: bfloat16 [3, 3, 3, 64, 64], replicated, may hold values from -0.15625 to 0.15625
- second_weight: bfloat16 [3, 3, 3, 64, 64], replicated, may hold values from -0.15625 to 0.15625
- brick_ids: int32 [512], P(('shape', 'grp')), parts along dimension 0, may hold values from -1 to 255, as said below
- brick_owner: int32 [512], P(('shape', 'grp')), parts along dimension 0, may hold values from -1 to 7, as said below
- neighbor_live: int32 [512, 27], P(('shape', 'grp')), parts along dimension 0, may hold values 0 or 1
Outputs:
- fine_bricks: bfloat16 [512, 32768], P(('shape', 'grp')), parts along dimension 0
The draws below stay inside these ranges and needn't reach their ends.
There are 4 independent parts, one for each index of `shape`. The reference program is written for one: setup_inputs(seed, part) draws one part's arguments, and reference() takes and returns one part's arrays. A program takes and returns all parts, laid end to end along the dimension named above; an argument that names none is the same for every part. Nothing has to cross between parts.
Inputs may be any that keep to these rules, and one draw needn't show every extreme that they name: `brick_ids`: each device's block of 16 entries lists distinct bricks of its own panel by local number (x slowest, z fastest), -1 for an unused entry; every block uses 16 - 16 // 2 to 16 entries at any positions, and some block uses all of them. `brick_owner`: -1 exactly where brick_ids is -1. Within one device's block no owner appears more than 2 times among used entries, and one owner appears exactly 2 times among the used entries of every block.
All inputs are finite; a program needn't handle non-finite values. No bound on the sum of `neighbor_live` on one device may be relied on, other than what follows from the above.
Results may differ from the reference program's by a relative error of at most 0.0052.
Values may be sent and summed in bfloat16 or wider, within the bound.
No kernel may reach another device: no remote copies, remote signals or barrier semaphores. Data moves between devices by JAX's collectives and lax.ppermute only.
A program may use at most 128 MiB of HBM per device.

```python
import jax
import jax.numpy as jnp
from jax import lax

C1 = 128
C2 = 64
BE = 8
HB = 4
G = 64
PX = 4
BPD = 16
SCAP = 2
OWN_ROWS = 16
OUT_ROWS = 128
GX = 32
BRICKS = 128
N_GRP = 8


def brick_lists(key):
    base_key = jax.random.fold_in(key, 4242)
    split_keys = jax.random.split(base_key, 6)
    panel_count = PX // HB * (G // HB) * (G // HB)
    used_counts = BPD - jax.random.randint(split_keys[0], (N_GRP,), 0, BPD // 2 + 1)
    full_device = jax.random.randint(split_keys[1], (), 0, N_GRP)
    used_counts = jnp.where(jnp.arange(N_GRP) == full_device, BPD, used_counts)
    hot_owner = jax.random.randint(split_keys[2], (), 0, N_GRP).astype(jnp.int32)
    other_owners = (jnp.arange((N_GRP - 1) * SCAP) // SCAP).astype(jnp.int32)
    other_owners = other_owners + (other_owners >= hot_owner).astype(jnp.int32)

    def per_device(cell_key, pool_key, order_key, used_count):
        brick_cells = jax.random.permutation(cell_key, panel_count)[:BPD]
        brick_cells = (brick_cells + (panel_count - 1 - brick_cells[0])) % panel_count
        chosen = jax.random.permutation(pool_key, other_owners)[:BPD - SCAP]
        owner_list = jnp.concatenate([jnp.full((SCAP,), hot_owner, jnp.int32), chosen.astype(jnp.int32)])
        slot_order = jax.random.permutation(order_key, BPD)
        used_slot = slot_order < used_count
        brick_list = jnp.where(used_slot, brick_cells[slot_order], -1)
        owner_slots = jnp.where(used_slot, owner_list[slot_order], -1)
        return (brick_list.astype(jnp.int32), owner_slots.astype(jnp.int32))
    brick_list, owner_slots = jax.vmap(per_device)(jax.random.split(split_keys[3], N_GRP), jax.random.split(split_keys[4], N_GRP), jax.random.split(split_keys[5], N_GRP), used_counts)
    return (brick_list.reshape(-1), owner_slots.reshape(-1))


def draw_brick_ids(key, part):
    return brick_lists(key)[0]


def draw_brick_owner(key, part):
    return brick_lists(key)[1]


def set_ends(values, key, least, top_value):
    longest = values.shape.index(max(values.shape))
    spots = []
    for shift in (0, 1):
        where = [jax.random.randint(jax.random.fold_in(key, axis), (), 0, length) for axis, length in enumerate(values.shape)]
        where[longest] = (where[longest] + shift) % values.shape[longest]
        spots.append(tuple(where))
    return values.at[spots[0]].set(least).at[spots[1]].set(top_value)


def levels(own_key, dims, shards, low, top_value):
    def one(position, parts):
        steps = jax.random.uniform(jax.random.fold_in(jax.random.fold_in(own_key, 6), position), (parts,), jnp.float32, low / len(shards), top_value / len(shards))
        return jnp.repeat(jnp.exp(steps), dims[position] // parts).reshape((-1,) + (1,) * (len(dims) - position - 1))

    level = one(*shards[0])
    for cut in shards[1:]:
        level = level * one(*cut)
    return level


def noise(key, dims, width, limit, cuts=(), kind=jnp.bfloat16):
    values = width * jax.random.normal(key, dims, jnp.float32)
    if cuts:
        values = values * levels(key, dims, cuts, -0.22, 0.18)
    return jnp.clip(values, -limit, limit).astype(kind)


def setup_inputs(seed: int = 0, part: int = 0) -> dict:
    streams_of = jax.random.split(jax.random.key(seed), 8)
    own_keys = jax.random.split(jax.random.fold_in(streams_of[7], part), 8)
    latents = noise(own_keys[0], (GX, G, G, C1), 1.0, 6.0, ((0, 8),))
    up_weight = noise(streams_of[1], (3, 3, 3, C1, C2), (4 * C1) ** -0.5, 0.25)
    first_weight = noise(streams_of[2], (3, 3, 3, C2, C2), (27 * C2) ** -0.5, 0.15625)
    second_weight = noise(streams_of[3], (3, 3, 3, C2, C2), (27 * C2) ** -0.5, 0.15625)
    brick_ids = draw_brick_ids(jax.random.fold_in(jax.random.fold_in(streams_of[7], part), 71), part)
    brick_owner = draw_brick_owner(jax.random.fold_in(jax.random.fold_in(streams_of[7], part), 71), part)
    neighbor_live = set_ends((jax.random.randint(own_keys[6], (BRICKS, 27), 0, 3) < 2).astype(jnp.int32), jax.random.fold_in(own_keys[6], 1), 0, 1)
    return dict(latents=latents, up_weight=up_weight, first_weight=first_weight, second_weight=second_weight, brick_ids=brick_ids, brick_owner=brick_owner, neighbor_live=neighbor_live)


parity_taps = (((1, 0),), ((2, 0), (0, 1)))


def upsample(regions, weight):
    sub_edge = regions.shape[1] - 1
    parity_grids = []
    for parity_x in range(2):
        plane_list = []
        for parity_y in range(2):
            line_list = []
            for parity_z in range(2):
                pieces = []
                kernels = []
                for tap_x, shift_x in parity_taps[parity_x]:
                    for tap_y, shift_y in parity_taps[parity_y]:
                        for tap_z, shift_z in parity_taps[parity_z]:
                            pieces.append(regions[:, shift_x:shift_x + sub_edge, shift_y:shift_y + sub_edge, shift_z:shift_z + sub_edge, :])
                            kernels.append(weight[tap_x, tap_y, tap_z])
                stacked = jnp.concatenate(pieces, axis=-1).astype(jnp.float32)
                kernel = jnp.concatenate(kernels, axis=0).astype(jnp.float32)
                line_list.append(jnp.einsum("bxyzc,co->bxyzo", stacked, kernel, precision=lax.Precision.HIGHEST))
            plane_list.append(jnp.stack(line_list, axis=4))
        parity_grids.append(jnp.stack(plane_list, axis=3))
    alternated = jnp.stack(parity_grids, axis=2)
    return alternated.reshape(regions.shape[0], 2 * sub_edge, 2 * sub_edge, 2 * sub_edge, weight.shape[-1])


def cell_mask(live_flags, full_edge):
    cell_pos = jnp.arange(full_edge, dtype=jnp.int32)
    neighbor_class = (cell_pos >= 2).astype(jnp.int32) + (cell_pos >= full_edge - 2).astype(jnp.int32)
    selector = (neighbor_class[:, None] == jnp.arange(3, dtype=jnp.int32)[None, :]).astype(jnp.float32)
    flag_cube = live_flags.reshape(live_flags.shape[0], 3, 3, 3)
    return jnp.einsum("bijk,xi,yj,zk->bxyz", flag_cube, selector, selector, selector, precision=lax.Precision.HIGHEST)


def conv_valid(inputs, kernel):
    return lax.conv_general_dilated(inputs.astype(jnp.float32), kernel.astype(jnp.float32), (1, 1, 1), "VALID", dimension_numbers=("NDHWC", "DHWIO", "NDHWC"), precision=lax.Precision.HIGHEST)


def refine(extended, full_mask, first_weight, second_weight):
    first_out = conv_valid(extended, first_weight)
    hidden = (jax.nn.silu(first_out) * full_mask[:, 1:-1, 1:-1, 1:-1, None]).astype(jnp.bfloat16)
    second_out = conv_valid(hidden, second_weight)
    refined = extended[:, 2:-2, 2:-2, 2:-2, :].astype(jnp.float32) + second_out
    return refined.astype(jnp.bfloat16).reshape(extended.shape[0], -1)


def neighbor_flags(brick_x, brick_y, brick_z, in_use, neighbor_live, bricks_long, bricks_across):
    offsets = jnp.arange(27, dtype=jnp.int32)
    step_x = offsets // 9 - 1
    step_y = (offsets // 3) % 3 - 1
    step_z = offsets % 3 - 1
    near_x = brick_x[:, None] + step_x[None, :]
    near_y = brick_y[:, None] + step_y[None, :]
    near_z = brick_z[:, None] + step_z[None, :]
    inside = (near_x >= 0) & (near_x < bricks_long) & (near_y >= 0) & (near_y < bricks_across) & (near_z >= 0) & (near_z < bricks_across)
    chosen = (neighbor_live > 0) | (offsets == 13)[None, :]
    return (inside & chosen & in_use[:, None]).astype(jnp.float32)


def reference(latents, up_weight, first_weight, second_weight, brick_ids, brick_owner, neighbor_live):
    across = G // HB
    panel_bricks = PX // HB
    padded = jnp.pad(latents, ((1, 2), (1, 2), (1, 2), (0, 0)))
    ids_block = brick_ids.reshape(N_GRP, BPD)
    owner_block = brick_owner.reshape(N_GRP, BPD)
    live_block = neighbor_live.reshape(N_GRP, BPD, 27)

    def one_device(inputs):
        device_pos, device_ids, device_live = inputs
        in_use = device_ids >= 0
        safe_ids = jnp.maximum(device_ids, 0).astype(jnp.int32)
        brick_x = (device_pos * panel_bricks + safe_ids // (across * across)).astype(jnp.int32)
        brick_y = ((safe_ids // across) % across).astype(jnp.int32)
        brick_z = (safe_ids % across).astype(jnp.int32)

        def slice_region(start_x, start_y, start_z):
            starts = ((start_x * HB).astype(jnp.int32), (start_y * HB).astype(jnp.int32), (start_z * HB).astype(jnp.int32), jnp.int32(0))
            return lax.dynamic_slice(padded, starts, (HB + 3, HB + 3, HB + 3, C1))

        regions = jax.vmap(slice_region)(brick_x, brick_y, brick_z)
        live_flags = neighbor_flags(brick_x, brick_y, brick_z, in_use, device_live, panel_bricks * N_GRP, across)
        full_mask = cell_mask(live_flags, BE + 4)
        extended = (upsample(regions, up_weight) * full_mask[..., None]).astype(jnp.bfloat16)
        return refine(extended, full_mask, first_weight, second_weight)

    refined_all = lax.map(one_device, (jnp.arange(N_GRP, dtype=jnp.int32), ids_block, live_block))
    in_use_all = ids_block >= 0
    owner_onehot = ((owner_block[:, :, None] == jnp.arange(N_GRP, dtype=jnp.int32)[None, None, :]) & in_use_all[:, :, None]).astype(jnp.int32)
    earlier = jnp.cumsum(owner_onehot, axis=1) - owner_onehot
    owner_rank = jnp.sum(earlier * owner_onehot, axis=2)
    target = owner_block * OWN_ROWS + jnp.arange(N_GRP, dtype=jnp.int32)[:, None] * SCAP + owner_rank
    target = jnp.where(in_use_all, target, OUT_ROWS)
    flat_rows = refined_all.reshape(N_GRP * BPD, -1)
    result = jnp.zeros((OUT_ROWS, flat_rows.shape[1]), jnp.bfloat16).at[target.reshape(-1)].set(flat_rows, mode="drop")
    return result
```

```python
import jax
import jax.numpy as jnp
from jax import lax
from jax.experimental import pallas as pl
from jax.experimental.pallas import tpu as pltpu
from jax.sharding import PartitionSpec as P

BE = 8
HB = 4
EDGE = HB + 3
WIN = 16

taps = (((1, 0),), ((2, 0), (0, 1)))


def slot_windows(slot_ids, grid):
    across = grid // HB
    slots = slot_ids.shape[0]
    safe = jnp.maximum(slot_ids, 0)
    low_y = safe // across % across * HB - 1
    low_z = safe % across * HB - 1
    start_y = jnp.clip(low_y, 0, grid - EDGE)
    start_z = jnp.clip(low_z // 8 * 8, 0, grid - WIN)
    starts = jnp.stack([start_y, low_y - start_y, start_z]).astype(jnp.int32)
    step = jnp.arange(EDGE, dtype=jnp.int32)
    place = jnp.arange(slots, dtype=jnp.int32)
    row = jnp.arange(WIN, dtype=jnp.int32)
    same = (place[:, None] == place[None, :]) & (slot_ids >= 0)[:, None]
    wanted = (low_z - start_z)[None, :] + step[:, None]
    hit = (
        same[None, None, :, :, None]
        & (row[None, None, None, None, :] == wanted[None, :, :, None, None])
    )
    inside = low_y + EDGE - 1 <= grid
    keep = jnp.stack([jnp.ones_like(inside), inside])
    hit = hit & keep[:, None, :, None, None]
    return starts, hit.astype(jnp.bfloat16).reshape(2, EDGE * slots, slots * WIN)


def gather(latents, jobs):
    grid = latents.shape[1]
    channels = latents.shape[3]
    slots = jobs[0][0].shape[0]
    prepared = [slot_windows(ids, grid) for ids, _, _ in jobs]
    starts = jnp.stack([one[0] for one in prepared])
    picks = jnp.stack([one[1] for one in prepared])

    def kernel(starts_ref, latents_ref, picks_ref, *refs):
        outs = refs[: len(jobs)]
        wins = refs[len(jobs) : 2 * len(jobs)]
        sems = refs[2 * len(jobs)]
        copies = []
        for job, (_, plane, count) in enumerate(jobs):
            for slot in range(slots):
                copy = pltpu.make_async_copy(
                    latents_ref.at[
                        pl.ds(plane, count),
                        pl.ds(starts_ref[job, 0, slot], EDGE),
                        pl.ds(pl.multiple_of(starts_ref[job, 2, slot], 8), WIN),
                        :,
                    ],
                    wins[job].at[slot],
                    sems.at[job, slot],
                )
                copy.start()
                copies.append(copy)
        for copy in copies:
            copy.wait()

        def line(y, carry):
            late = (y >= EDGE - 2).astype(jnp.int32)
            for job, (_, _, count) in enumerate(jobs):
                rows = []
                for slot in range(slots):
                    rows.append(jnp.clip(y + starts_ref[job, 1, slot], 0, EDGE - 1))
                planes = []
                for x in range(count):
                    planes.append(
                        jnp.concatenate(
                            [wins[job][slot, x, rows[slot]] for slot in range(slots)], axis=0
                        )
                    )
                block = jnp.concatenate(planes, axis=1)
                cut = jnp.dot(
                    picks_ref[job, late], block, preferred_element_type=jnp.float32
                ).astype(jnp.bfloat16)
                for x in range(count):
                    outs[job][x, y] = cut[:, x * channels : (x + 1) * channels].reshape(
                        EDGE, slots, channels
                    )
            return carry

        lax.fori_loop(0, EDGE, line, 0)

    vmem = pl.BlockSpec(memory_space=pltpu.VMEM)
    return pl.pallas_call(
        kernel,
        in_specs=[
            pl.BlockSpec(memory_space=pltpu.SMEM),
            pl.BlockSpec(memory_space=pl.ANY),
            vmem,
        ],
        out_specs=[vmem] * len(jobs),
        out_shape=[
            jax.ShapeDtypeStruct((count, EDGE, EDGE, slots, channels), jnp.bfloat16)
            for _, _, count in jobs
        ],
        scratch_shapes=[
            pltpu.VMEM((slots, count, EDGE, WIN, channels), jnp.bfloat16)
            for _, _, count in jobs
        ]
        + [pltpu.SemaphoreType.DMA((len(jobs), slots))],
        compiler_params=pltpu.CompilerParams(vmem_limit_bytes=48 << 20),
        cost_estimate=pl.CostEstimate(
            flops=100_000_000, bytes_accessed=4_000_000, transcendentals=0
        ),
    )(starts, latents, picks)


def paired_up(weight):
    depth, width = weight.shape[3:]
    zero = jnp.zeros((3, depth, width), weight.dtype)
    lookup = {(parity, shift): tap for parity in (0, 1) for tap, shift in taps[parity]}
    rows = []
    for dy in (0, 1):
        for dz in (0, 1):
            cols = []
            for py in (0, 1):
                for pz in (0, 1):
                    ty = lookup.get((py, dy))
                    tz = lookup.get((pz, dz))
                    cols.append(zero if ty is None or tz is None else weight[:, ty, tz])
            rows.append(jnp.concatenate(cols, axis=2))
    return jnp.concatenate(rows, axis=1)


def paired_conv(weight):
    depth, width = weight.shape[3:]
    zero = jnp.zeros((3, depth, width), weight.dtype)
    rows = []
    for dy in (0, 1):
        for dz in (0, 1):
            for iy in (0, 1):
                for iz in (0, 1):
                    cols = []
                    for oy in (0, 1):
                        for oz in (0, 1):
                            ky = 2 * dy + iy - oy
                            kz = 2 * dz + iz - oz
                            inside = 0 <= ky <= 2 and 0 <= kz <= 2
                            cols.append(weight[:, ky, kz] if inside else zero)
                    rows.append(jnp.concatenate(cols, axis=2))
    return jnp.concatenate(rows, axis=1).reshape(-1, 4 * width)


def decode(low, own, high, live, up_pairs, first_pairs, second_pairs):
    slots = own.shape[3]
    c1 = own.shape[4]
    quad = up_pairs.shape[2]
    c2 = quad // 4
    epairs = BE // 2 + 2
    hpairs = BE // 2 + 1
    opairs = BE // 2
    eedge = BE + 4
    hedge = BE + 2

    def kernel(low_ref, own_ref, high_ref, live_ref, up_ref, first_ref, second_ref, out_ref,
               reg, ext, hid, emask, hmask):
        reg[0] = low_ref[0]
        reg[1 : 1 + HB] = own_ref[...]
        reg[1 + HB : 3 + HB] = high_ref[...]
        flags = live_ref[...]
        wide = [
            jnp.broadcast_to(flags[:, n : n + 1], (slots, 2 * c2)).astype(jnp.float32)
            for n in range(27)
        ]
        left = lax.broadcasted_iota(jnp.int32, (slots, 2 * c2), 1) < c2

        def pair_class(p):
            return 0 if p == 0 else 2 if p == epairs - 1 else 1

        def cell_class(h):
            return 0 if h == 0 else 2 if h == hedge - 1 else 1

        for cx in range(3):
            for py in range(epairs):
                for pz in range(epairs):
                    n = cx * 9 + pair_class(py) * 3 + pair_class(pz)
                    emask[cx, py, pz] = wide[n].astype(jnp.bfloat16)
            for py in range(hpairs):
                for pz in range(hpairs):
                    for ty in (0, 1):
                        n = cx * 9 + cell_class(2 * py + ty) * 3
                        both = jnp.where(
                            left,
                            wide[n + cell_class(2 * pz)],
                            wide[n + cell_class(2 * pz + 1)],
                        )
                        hmask[cx, py, pz, :, ty * 2 * c2 : (ty + 1) * 2 * c2] = both.astype(
                            jnp.bfloat16
                        )

        def up(px, carry):
            def patch(x):
                return jnp.concatenate(
                    [
                        reg[x, dy : dy + epairs, dz : dz + epairs].reshape(-1, c1)
                        for dy in (0, 1)
                        for dz in (0, 1)
                    ],
                    axis=1,
                )

            cx = jnp.where(px == 0, 0, jnp.where(px == epairs - 1, 2, 1))
            mask = emask[cx].reshape(-1, 2 * c2)
            mask = jnp.concatenate([mask, mask], axis=1)
            first = patch(px)
            even = jnp.dot(first, up_ref[1], preferred_element_type=jnp.float32)
            ext[2 * px] = (even.astype(jnp.bfloat16) * mask).reshape(epairs, epairs, slots, quad)
            odd = jnp.dot(first, up_ref[2], preferred_element_type=jnp.float32)
            odd += jnp.dot(patch(px + 1), up_ref[0], preferred_element_type=jnp.float32)
            ext[2 * px + 1] = (odd.astype(jnp.bfloat16) * mask).reshape(
                epairs, epairs, slots, quad
            )
            return carry

        lax.fori_loop(0, epairs, up, 0)

        def conv(source, x, pairs, weight_ref):
            pieces = [
                source[x + kx, dy : dy + pairs, dz : dz + pairs].reshape(-1, quad)
                for kx in range(3)
                for dy in (0, 1)
                for dz in (0, 1)
            ]
            return jnp.dot(
                jnp.concatenate(pieces, axis=1),
                weight_ref[...],
                preferred_element_type=jnp.float32,
            )

        def first(x, carry):
            value = conv(ext, x, hpairs, first_ref)
            cx = jnp.where(x == 0, 0, jnp.where(x == hedge - 1, 2, 1))
            value = (value * (1.0 / (1.0 + jnp.exp(-value)))).astype(jnp.bfloat16)
            value = value * hmask[cx].reshape(-1, quad)
            hid[x] = value.reshape(hpairs, hpairs, slots, quad)
            return carry

        lax.fori_loop(0, hedge, first, 0)

        def second(x, carry):
            value = conv(hid, x, opairs, second_ref)
            centre = ext[x + 2, 1 : 1 + opairs, 1 : 1 + opairs].reshape(-1, quad)
            value = (value + centre.astype(jnp.float32)).astype(jnp.bfloat16)
            value = value.reshape(opairs, opairs, slots, quad)
            base = pl.multiple_of(x * (BE * BE * c2), 128)
            for py in range(opairs):
                for ty in (0, 1):
                    line = jnp.concatenate(
                        [
                            value[py, pz, :, ty * 2 * c2 : (ty + 1) * 2 * c2]
                            for pz in range(opairs)
                        ],
                        axis=1,
                    )
                    shift = (2 * py + ty) * BE * c2
                    out_ref[:, pl.ds(pl.multiple_of(base + shift, 128), BE * c2)] = line
            return carry

        lax.fori_loop(0, BE, second, 0)

    vmem = pl.BlockSpec(memory_space=pltpu.VMEM)
    return pl.pallas_call(
        kernel,
        in_specs=[vmem] * 7,
        out_specs=vmem,
        out_shape=jax.ShapeDtypeStruct((slots, BE * BE * BE * c2), jnp.bfloat16),
        scratch_shapes=[
            pltpu.VMEM((EDGE, EDGE, EDGE, slots, c1), jnp.bfloat16),
            pltpu.VMEM((eedge, epairs, epairs, slots, quad), jnp.bfloat16),
            pltpu.VMEM((hedge, hpairs, hpairs, slots, quad), jnp.bfloat16),
            pltpu.VMEM((3, epairs, epairs, slots, 2 * c2), jnp.bfloat16),
            pltpu.VMEM((3, hpairs, hpairs, slots, quad), jnp.bfloat16),
        ],
        compiler_params=pltpu.CompilerParams(vmem_limit_bytes=56 << 20),
        cost_estimate=pl.CostEstimate(
            flops=12_000_000_000, bytes_accessed=8_000_000, transcendentals=1_000_000
        ),
    )(low, own, high, live, up_pairs, first_pairs, second_pairs)


def neighbor_flags(brick_x, brick_y, brick_z, in_use, neighbor_live, bricks_long, bricks_across):
    offsets = jnp.arange(27, dtype=jnp.int32)
    step_x = offsets // 9 - 1
    step_y = offsets // 3 % 3 - 1
    step_z = offsets % 3 - 1
    near_x = brick_x + step_x[None, :]
    near_y = brick_y[:, None] + step_y[None, :]
    near_z = brick_z[:, None] + step_z[None, :]
    inside = (
        (near_x >= 0)
        & (near_x < bricks_long)
        & (near_y >= 0)
        & (near_y < bricks_across)
        & (near_z >= 0)
        & (near_z < bricks_across)
    )
    chosen = (neighbor_live > 0) | (offsets == 13)[None, :]
    return (inside & chosen & in_use[:, None]).astype(jnp.int32)


def exchange(windows, group, shift):
    lead = windows.shape[:3]
    slots, channels = windows.shape[3:]
    split = windows.reshape(-1, group, slots // group, channels)
    moved = lax.all_to_all(split, "grp", split_axis=1, concat_axis=1, tiled=True)
    if shift:
        moved = jnp.roll(moved, shift, axis=1)
    return moved.reshape(*lead, slots, channels)


def local(latents, up_weight, first_weight, second_weight, brick_ids, brick_owner, neighbor_live):
    group = lax.axis_size("grp")
    me = lax.axis_index("grp")
    listed = brick_ids.shape[0]
    capacity = max(2, listed // group)
    slots = group * capacity
    grid = latents.shape[1]
    across = grid // HB
    assert latents.shape[0] == HB

    in_use = brick_ids >= 0
    safe_ids = jnp.maximum(brick_ids, 0)
    entry = jnp.arange(listed, dtype=jnp.int32)
    before = (
        (brick_owner[:, None] == brick_owner[None, :])
        & in_use[None, :]
        & (entry[None, :] < entry[:, None])
    )
    rank = jnp.sum(before.astype(jnp.int32), axis=1)
    target = jnp.where(in_use, brick_owner * capacity + rank, slots)
    chosen = (target[None, :] == jnp.arange(slots, dtype=jnp.int32)[:, None]).astype(jnp.int32)
    slot_ids = jnp.sum(chosen * (brick_ids[None, :] + 1), axis=1) - 1
    flags = neighbor_flags(
        me, safe_ids // across % across, safe_ids % across, in_use, neighbor_live, group, across
    )
    slot_flags = jnp.sum(chosen[:, :, None] * flags[None, :, :], axis=1)

    message = jnp.concatenate(
        [jnp.broadcast_to(slot_ids, (group, slots)), slot_flags.reshape(group, capacity * 27)],
        axis=1,
    )
    heard = lax.all_to_all(message, "grp", split_axis=0, concat_axis=0, tiled=True)
    live = heard[:, slots:].reshape(slots, 27)
    ids_of = heard[:, :slots]
    below = lax.dynamic_index_in_dim(ids_of, (me + group - 1) % group, 0, keepdims=False)
    above = lax.dynamic_index_in_dim(ids_of, (me + 1) % group, 0, keepdims=False)
    below = jnp.where(me > 0, below, -1)
    above = jnp.where(me < group - 1, above, -1)

    (own,) = gather(latents, [(slot_ids, 0, HB)])
    high, low = gather(latents, [(below, 0, 2), (above, HB - 1, 1)])
    own = exchange(own, group, 0)
    high = exchange(high, group, -1)
    low = exchange(low, group, 1)
    return decode(
        low, own, high, live,
        paired_up(up_weight), paired_conv(first_weight), paired_conv(second_weight),
    )


def solution(mesh):
    in_specs = (
        P(("shape", "grp"), None, None, None),
        P(),
        P(),
        P(),
        P(("shape", "grp")),
        P(("shape", "grp")),
        P(("shape", "grp"), None),
    )
    out_specs = P(("shape", "grp"), None)
    return jax.shard_map(local, mesh=mesh, in_specs=in_specs, out_specs=out_specs, check_vma=False)
```

```python
import jax
import jax.numpy as jnp
from jax import lax
from jax.experimental import pallas as pl
from jax.experimental.pallas import tpu as pltpu
from jax.sharding import PartitionSpec as P


BE = 8
HB = 4
EDGE = HB + 3
WIN = 16
FAR = -1000
BIG = 65_536_000

EEDGE = BE + 4
HEDGE = BE + 2
EP = EEDGE // 2
HP = HEDGE // 2
OP = BE // 2

taps = (((1, 0),), ((2, 0), (0, 1)))

VMEM = pl.BlockSpec(memory_space=pltpu.VMEM)
SMEM = pl.BlockSpec(memory_space=pltpu.SMEM)
HBM = pl.BlockSpec(memory_space=pltpu.HBM)


def cost(flops, moved):
    return pl.CostEstimate(flops=flops, bytes_accessed=moved, transcendentals=0)


def window_of(brick, grid):
    across = grid // HB
    safe = jnp.maximum(brick, 0)
    along_y = lax.rem(lax.div(safe, across), across)
    low_y = along_y * HB - 1
    low_z = lax.rem(safe, across) * HB - 1
    start_y = jnp.clip(low_y, 0, grid - EDGE)
    start_z = jnp.clip(lax.div(low_z + 8, 8) * 8 - 8, 0, grid - WIN)
    return start_y, low_y - start_y, start_z, low_z - start_z, along_y == across - 1


def cut_windows(bricks, latents_ref, plane, count, win, sem, pick, out_ref, base):
    grid = latents_ref.shape[1]
    channels = latents_ref.shape[3]
    slots = len(bricks)
    group, _, capacity, _ = out_ref.shape
    places = [window_of(brick, grid) for brick in bricks]
    copies = []
    for slot, (start_y, _, start_z, _, _) in enumerate(places):
        copy = pltpu.make_async_copy(
            latents_ref.at[
                pl.ds(plane, count),
                pl.ds(start_y, EDGE),
                pl.ds(pl.multiple_of(start_z, 8), WIN),
                :,
            ],
            win.at[slot],
            sem.at[slot],
        )
        copy.start()
        copies.append(copy)

    def finish():
        shape = (EDGE * slots, slots * WIN)
        column = lax.broadcasted_iota(jnp.int32, (1, slots * WIN), 1)
        shift = jnp.full((1, slots * WIN), FAR, jnp.int32)
        late = shift
        for slot, (_, _, _, shift_z, top) in enumerate(places):
            here = column // WIN == slot
            value = jnp.where(bricks[slot] >= 0, shift_z, FAR)
            shift = jnp.where(here, value, shift)
            late = jnp.where(here, jnp.where(top, FAR, value), late)
        row = lax.broadcasted_iota(jnp.int32, shape, 0)
        column = lax.broadcasted_iota(jnp.int32, shape, 1)
        same = row % slots == column // WIN
        step = column % WIN - row // slots
        pick[0] = jnp.where(same & (step == shift), 1.0, 0.0).astype(jnp.bfloat16)
        pick[1] = jnp.where(same & (step == late), 1.0, 0.0).astype(jnp.bfloat16)
        for copy in copies:
            copy.wait()

        def line(y, carry):
            rows = [jnp.clip(y + place[1], 0, EDGE - 1) for place in places]
            planes = [
                jnp.concatenate([win[slot, x, rows[slot]] for slot in range(slots)], axis=0)
                for x in range(count)
            ]
            cut = jnp.dot(
                pick[(y >= EDGE - 2).astype(jnp.int32)],
                jnp.concatenate(planes, axis=1),
                preferred_element_type=jnp.float32,
            ).astype(jnp.bfloat16)
            for x in range(count):
                for z in range(EDGE):
                    out_ref[:, base + (x * EDGE + y) * EDGE + z] = cut[
                        z * slots : (z + 1) * slots, x * channels : (x + 1) * channels
                    ].reshape(group, capacity, channels)
            return carry

        lax.fori_loop(0, EDGE, line, 0)

    return finish


def gather_own(latents, brick_ids, brick_owner, neighbor_live, group, capacity):
    grid = latents.shape[1]
    channels = latents.shape[3]
    across = grid // HB
    listed = brick_ids.shape[0]
    slots = group * capacity
    cells = HB * EDGE * EDGE

    def kernel(ids_ref, owner_ref, near_ref, latents_ref, out_ref, ids_out, entry_of, used_by,
               flags, win, pick, sem):
        me = lax.axis_index("grp")
        for slot in range(slots):
            entry_of[slot] = -1
        for owner in range(group):
            used_by[owner] = 0
        for entry in range(listed):
            owner = jnp.clip(owner_ref[entry], 0, group - 1)
            rank = used_by[owner]

            @pl.when((ids_ref[entry] >= 0) & (rank < capacity))
            def _():
                entry_of[owner * capacity + rank] = entry
                used_by[owner] = rank + 1

        entries = [entry_of[slot] for slot in range(slots)]
        bricks = [
            jnp.where(entry >= 0, ids_ref[jnp.maximum(entry, 0)], -1) for entry in entries
        ]
        finish = cut_windows(bricks, latents_ref, 0, HB, win, sem, pick, out_ref, 0)

        lane = lax.broadcasted_iota(jnp.int32, (1, 128), 1)
        told = jnp.full((1, 128), -1, jnp.int32)
        for slot in range(slots):
            told = jnp.where(lane == slot, bricks[slot], told)
        for owner in range(group):
            ids_out[owner] = told

        offset = lax.broadcasted_iota(jnp.int32, (1, 27), 1)
        step_x = offset // 9 - 1
        step_y = offset // 3 % 3 - 1
        step_z = offset % 3 - 1
        inside_x = (me + step_x >= 0) & (me + step_x < group)
        flags[...] = jnp.zeros_like(flags)
        for slot in range(slots):
            safe = jnp.maximum(bricks[slot], 0)
            near_y = lax.rem(lax.div(safe, across), across) + step_y
            near_z = lax.rem(safe, across) + step_z
            inside = inside_x & (near_y >= 0) & (near_y < across)
            inside = inside & (near_z >= 0) & (near_z < across)
            near = near_ref[pl.ds(jnp.maximum(entries[slot], 0), 1), :]
            chosen = (near > 0) | (offset == 13)
            used = jnp.where(bricks[slot] >= 0, 1.0, 0.0)
            flags[slot : slot + 1, 0:27] = jnp.where(inside & chosen, used, 0.0)
        out_ref[:, cells] = flags[...].astype(jnp.bfloat16).reshape(group, capacity, channels)
        finish()

    return pl.pallas_call(
        kernel,
        in_specs=[SMEM, SMEM, VMEM, HBM],
        out_specs=[VMEM, VMEM],
        out_shape=[
            jax.ShapeDtypeStruct((group, cells + 1, capacity, channels), jnp.bfloat16),
            jax.ShapeDtypeStruct((group, 1, 128), jnp.int32),
        ],
        scratch_shapes=[
            pltpu.SMEM((slots,), jnp.int32),
            pltpu.SMEM((group,), jnp.int32),
            pltpu.VMEM((slots, 128), jnp.float32),
            pltpu.VMEM((slots, HB, EDGE, WIN, channels), jnp.bfloat16),
            pltpu.VMEM((2, EDGE * slots, slots * WIN), jnp.bfloat16),
            pltpu.SemaphoreType.DMA((slots,)),
        ],
        compiler_params=pltpu.CompilerParams(vmem_limit_bytes=BIG),
        cost_estimate=cost(1_000_000_000, 3_000_000),
    )(brick_ids, brick_owner, neighbor_live, latents)


def gather_rims(latents, heard, group, capacity):
    channels = latents.shape[3]
    slots = group * capacity
    plane_cells = EDGE * EDGE

    def kernel(heard_ref, latents_ref, out_ref, win_b, win_a, pick_b, pick_a, sem):
        me = lax.axis_index("grp")
        before = lax.rem(me + group - 1, group)
        after = lax.rem(me + 1, group)
        below = [jnp.where(me > 0, heard_ref[before, 0, slot], -1) for slot in range(slots)]
        above = [
            jnp.where(me < group - 1, heard_ref[after, 0, slot], -1) for slot in range(slots)
        ]
        finish_b = cut_windows(below, latents_ref, 0, 2, win_b, sem.at[0], pick_b, out_ref, 0)
        finish_a = cut_windows(
            above, latents_ref, HB - 1, 1, win_a, sem.at[1], pick_a, out_ref, 2 * plane_cells
        )
        finish_b()
        finish_a()

    return pl.pallas_call(
        kernel,
        in_specs=[SMEM, HBM],
        out_specs=VMEM,
        out_shape=jax.ShapeDtypeStruct(
            (group, 3 * plane_cells, capacity, channels), jnp.bfloat16
        ),
        scratch_shapes=[
            pltpu.VMEM((slots, 2, EDGE, WIN, channels), jnp.bfloat16),
            pltpu.VMEM((slots, 1, EDGE, WIN, channels), jnp.bfloat16),
            pltpu.VMEM((2, EDGE * slots, slots * WIN), jnp.bfloat16),
            pltpu.VMEM((2, EDGE * slots, slots * WIN), jnp.bfloat16),
            pltpu.SemaphoreType.DMA((2, slots)),
        ],
        compiler_params=pltpu.CompilerParams(vmem_limit_bytes=BIG),
        cost_estimate=cost(1_000_000_000, 3_000_000),
    )(heard, latents)


def pair_weights(up_weight, first_weight, second_weight, after):
    c1, c2 = up_weight.shape[3:]
    quad = 4 * c2
    lookup = {(parity, shift): tap for parity in (0, 1) for tap, shift in taps[parity]}

    def kernel(up_ref, first_ref, second_ref, after_ref, up_hbm, first_hbm, second_hbm,
               up_out, first_out, second_out, sem):
        moves = [
            pltpu.make_async_copy(source, target, sem.at[i])
            for i, (source, target) in enumerate(
                ((up_out, up_hbm), (first_out, first_hbm), (second_out, second_hbm))
            )
        ]
        for kx in range(3):
            for dy in (0, 1):
                for dz in (0, 1):
                    for py in (0, 1):
                        both = []
                        for pz in (0, 1):
                            ty = lookup.get((py, dy))
                            tz = lookup.get((pz, dz))
                            both.append(
                                jnp.zeros((c1, c2), jnp.bfloat16)
                                if ty is None or tz is None
                                else up_ref[kx, ty, tz]
                            )
                        at = (dy * 2 + dz) * c1
                        up_out[kx, at : at + c1, py * 2 * c2 : (py + 1) * 2 * c2] = (
                            jnp.concatenate(both, axis=1)
                        )
        moves[0].start()
        for raw, out, move in (
            (first_ref, first_out, moves[1]),
            (second_ref, second_out, moves[2]),
        ):
            def tile(kx, carry, raw=raw, out=out):
                for dy in (0, 1):
                    for dz in (0, 1):
                        for iy in (0, 1):
                            for iz in (0, 1):
                                for oy in (0, 1):
                                    both = []
                                    for oz in (0, 1):
                                        ky = 2 * dy + iy - oy
                                        kz = 2 * dz + iz - oz
                                        both.append(
                                            raw[kx, ky, kz]
                                            if 0 <= ky <= 2 and 0 <= kz <= 2
                                            else jnp.zeros((c2, c2), jnp.bfloat16)
                                        )
                                    at = (dy * 2 + dz) * quad + (iy * 2 + iz) * c2
                                    at = pl.multiple_of(kx * 4 * quad + at, c2)
                                    out[pl.ds(at, c2), oy * 2 * c2 : (oy + 1) * 2 * c2] = (
                                        jnp.concatenate(both, axis=1)
                                    )
                return carry

            lax.fori_loop(0, 3, tile, 0)
            move.start()
        for move in moves:
            move.wait()

    shapes = ((3, 4 * c1, quad), (12 * quad, quad), (12 * quad, quad))
    return pl.pallas_call(
        kernel,
        in_specs=[VMEM, VMEM, VMEM, HBM],
        out_specs=[HBM] * 3,
        out_shape=[jax.ShapeDtypeStruct(shape, jnp.bfloat16) for shape in shapes],
        scratch_shapes=[pltpu.VMEM(shape, jnp.bfloat16) for shape in shapes]
        + [pltpu.SemaphoreType.DMA((3,))],
        compiler_params=pltpu.CompilerParams(vmem_limit_bytes=BIG),
        cost_estimate=cost(1_000_000_000, 6_000_000),
    )(up_weight, first_weight, second_weight, after)


def pair_class(p):
    return 0 if p == 0 else 2 if p == EP - 1 else 1


def cell_class(h):
    return 0 if h == 0 else 2 if h == HEDGE - 1 else 1


class Decoder:
    def __init__(self, slots, c1, quad):
        self.slots, self.c1, self.quad = slots, c1, quad

    def scratch(self):
        slots, quad = self.slots, self.quad
        return [
            pltpu.VMEM((EDGE, EDGE, EDGE, slots, self.c1), jnp.bfloat16),
            pltpu.VMEM((EEDGE, EP, EP, slots, quad), jnp.bfloat16),
            pltpu.VMEM((HEDGE, HP, HP, slots, quad), jnp.bfloat16),
            pltpu.VMEM((3, EP, EP, slots, quad // 2), jnp.bfloat16),
            pltpu.VMEM((3, HP, HP, slots, quad), jnp.bfloat16),
            pltpu.VMEM((slots, self.c1), jnp.float32),
            pltpu.VMEM((3, 4 * self.c1, quad), jnp.bfloat16),
            pltpu.VMEM((12 * quad, quad), jnp.bfloat16),
            pltpu.VMEM((12 * quad, quad), jnp.bfloat16),
            pltpu.SemaphoreType.DMA((3,)),
        ]

    @staticmethod
    def fetch(sources, targets, sem):
        moves = [
            pltpu.make_async_copy(source, target, sem.at[i])
            for i, (source, target) in enumerate(zip(sources, targets))
        ]
        for move in moves:
            move.start()
        return moves

    def masks(self, flags, emask, hmask, classes):
        half, c2 = self.quad // 2, self.quad // 4
        wide = {
            cx * 9 + n: jnp.broadcast_to(flags[:, cx * 9 + n : cx * 9 + n + 1], (self.slots, half))
            for cx in classes
            for n in range(9)
        }
        left = lax.broadcasted_iota(jnp.int32, (self.slots, half), 1) < c2
        for cx in classes:
            for py in range(EP):
                for pz in range(EP):
                    n = cx * 9 + pair_class(py) * 3 + pair_class(pz)
                    emask[cx, py, pz] = wide[n].astype(jnp.bfloat16)
            mixed = {}
            for py in range(HP):
                for pz in range(HP):
                    for ty in (0, 1):
                        n = cx * 9 + cell_class(2 * py + ty) * 3
                        key = (n + cell_class(2 * pz), n + cell_class(2 * pz + 1))
                        if key not in mixed:
                            mixed[key] = jnp.where(left, wide[key[0]], wide[key[1]]).astype(
                                jnp.bfloat16
                            )
                        hmask[cx, py, pz, :, ty * half : (ty + 1) * half] = mixed[key]

    def patch(self, reg, x):
        return jnp.concatenate(
            [
                reg[x, dy : dy + EP, dz : dz + EP].reshape(-1, self.c1)
                for dy in (0, 1)
                for dz in (0, 1)
            ],
            axis=1,
        )

    def raise_cells(self, reg, up_ref, emask, ext, px, parities):
        cx = jnp.where(px == 0, 0, jnp.where(px == EP - 1, 2, 1))
        mask = emask[cx].reshape(-1, self.quad // 2)
        mask = jnp.concatenate([mask, mask], axis=1)
        shape = (EP, EP, self.slots, self.quad)
        near = self.patch(reg, px)
        if 0 in parities:
            even = jnp.dot(near, up_ref[1], preferred_element_type=jnp.float32)
            ext[2 * px] = (even.astype(jnp.bfloat16) * mask).reshape(shape)
        if 1 in parities:
            odd = jnp.dot(near, up_ref[2], preferred_element_type=jnp.float32)
            odd += jnp.dot(self.patch(reg, px + 1), up_ref[0], preferred_element_type=jnp.float32)
            ext[2 * px + 1] = (odd.astype(jnp.bfloat16) * mask).reshape(shape)

    def conv(self, source, x, pairs, weight_ref):
        pieces = [
            source[x + kx, dy : dy + pairs, dz : dz + pairs].reshape(-1, self.quad)
            for kx in range(3)
            for dy in (0, 1)
            for dz in (0, 1)
        ]
        return jnp.dot(
            jnp.concatenate(pieces, axis=1), weight_ref[...], preferred_element_type=jnp.float32
        )

    def hide(self, ext, first_ref, hmask, hid, x):
        value = self.conv(ext, x, HP, first_ref)
        cx = jnp.where(x == 0, 0, jnp.where(x == HEDGE - 1, 2, 1))
        value = (value * (1.0 / (1.0 + jnp.exp(-value)))).astype(jnp.bfloat16)
        value = value * hmask[cx].reshape(-1, self.quad)
        hid[x] = value.reshape(HP, HP, self.slots, self.quad)

    def refine(self, ext, hid, second_ref, rows, x, at):
        half = self.quad // 2
        value = self.conv(hid, x, OP, second_ref)
        centre = ext[x + 2, 1 : 1 + OP, 1 : 1 + OP].reshape(-1, self.quad)
        value = (value + centre.astype(jnp.float32)).astype(jnp.bfloat16)
        value = value.reshape(OP, OP, self.slots, self.quad)
        for py in range(OP):
            for ty in (0, 1):
                line = jnp.concatenate(
                    [value[py, pz, :, ty * half : (ty + 1) * half] for pz in range(OP)], axis=1
                )
                start = pl.multiple_of(at * BE * OP * half + (2 * py + ty) * OP * half, 128)
                rows[:, pl.ds(start, OP * half)] = line


INNER_H, INNER_O = (2, 7), (2, 5)
KEPT_E = (2, 3, 7, 8)
KEPT_H = (2, 3, 5, 6)


def decode_inner(own, up_pairs, first_pairs, second_pairs):
    group, _, capacity, c1 = own.shape
    quad = up_pairs.shape[2]
    slots = group * capacity
    plane = BE * BE * quad // 4
    steps = Decoder(slots, c1, quad)
    width = (INNER_O[1] - INNER_O[0]) * plane

    def kernel(own_ref, up_in, first_in, second_in, out_ref, ext_out, hid_out,
               reg, ext, hid, emask, hmask, flags, up_ref, first_ref, second_ref, wsem, rows, sem):
        weights = steps.fetch(
            (up_in, first_in, second_in), (up_ref, first_ref, second_ref), wsem
        )
        flags[...] = own_ref[:, HB * EDGE * EDGE].reshape(slots, c1).astype(jnp.float32)

        def load(y, carry):
            for x in range(HB):
                for z in range(EDGE):
                    reg[1 + x, y, z] = own_ref[:, (x * EDGE + y) * EDGE + z].reshape(slots, c1)
            return carry

        lax.fori_loop(0, EDGE, load, 0)
        steps.masks(flags, emask, hmask, (1,))
        weights[0].wait()

        def both(px, carry):
            steps.raise_cells(reg, up_ref, emask, ext, px, (0, 1))
            return carry

        lax.fori_loop(1, HB, both, 0)
        steps.raise_cells(reg, up_ref, emask, ext, HB, (0,))
        copies = [
            pltpu.make_async_copy(ext.at[e], ext_out.at[i], sem.at[i])
            for i, e in enumerate(KEPT_E)
        ]
        for copy in copies:
            copy.start()

        weights[1].wait()

        def hide(x, carry):
            steps.hide(ext, first_ref, hmask, hid, x)
            return carry

        lax.fori_loop(INNER_H[0], INNER_H[1], hide, 0)
        more = [
            pltpu.make_async_copy(hid.at[h], hid_out.at[i], sem.at[4 + i])
            for i, h in enumerate(KEPT_H)
        ]
        for copy in more:
            copy.start()

        weights[2].wait()

        def refine(x, carry):
            steps.refine(ext, hid, second_ref, rows, x, x - INNER_O[0])
            return carry

        lax.fori_loop(INNER_O[0], INNER_O[1], refine, 0)
        last = pltpu.make_async_copy(
            rows, out_ref.at[:, pl.ds(INNER_O[0] * plane, width)], sem.at[8]
        )
        last.start()
        for copy in copies + more + [last]:
            copy.wait()

    return pl.pallas_call(
        kernel,
        in_specs=[VMEM] + [HBM] * 3,
        out_specs=[HBM] * 3,
        out_shape=[
            jax.ShapeDtypeStruct((slots, BE * plane), jnp.bfloat16),
            jax.ShapeDtypeStruct((len(KEPT_E), EP, EP, slots, quad), jnp.bfloat16),
            jax.ShapeDtypeStruct((len(KEPT_H), HP, HP, slots, quad), jnp.bfloat16),
        ],
        scratch_shapes=steps.scratch()
        + [pltpu.VMEM((slots, width), jnp.bfloat16), pltpu.SemaphoreType.DMA((9,))],
        compiler_params=pltpu.CompilerParams(vmem_limit_bytes=64_000_000),
        cost_estimate=cost(8_000_000_000, 6_000_000),
    )(own, up_pairs, first_pairs, second_pairs)


def decode_outer(own, rims, out, ext_kept, hid_kept, up_pairs, first_pairs, second_pairs):
    group, _, capacity, c1 = own.shape
    quad = up_pairs.shape[2]
    slots = group * capacity
    plane = BE * BE * quad // 4
    steps = Decoder(slots, c1, quad)
    plane_cells = EDGE * EDGE
    low_o = INNER_O[0]
    high_o = BE - INNER_O[1]

    def kernel(own_ref, rims_ref, up_in, first_in, second_in, ext_in, hid_in, out_in, out_ref,
               reg, ext, hid, emask, hmask, flags, up_ref, first_ref, second_ref, wsem, rows, sem):
        weights = steps.fetch(
            (up_in, first_in, second_in), (up_ref, first_ref, second_ref), wsem
        )
        copies = [
            pltpu.make_async_copy(ext_in.at[i], ext.at[e], sem.at[i])
            for i, e in enumerate(KEPT_E)
        ] + [
            pltpu.make_async_copy(hid_in.at[i], hid.at[h], sem.at[4 + i])
            for i, h in enumerate(KEPT_H)
        ]
        for copy in copies:
            copy.start()
        flags[...] = own_ref[:, HB * plane_cells].reshape(slots, c1).astype(jnp.float32)

        def turned(row, shift):
            value = rims_ref[:, row].reshape(slots, c1)
            cut = (shift % group) * capacity
            return jnp.concatenate([value[cut:], value[:cut]], axis=0)

        def load(y, carry):
            for z in range(EDGE):
                at = y * EDGE + z
                reg[0, y, z] = turned(2 * plane_cells + at, -1)
                reg[1, y, z] = own_ref[:, at].reshape(slots, c1)
                reg[HB, y, z] = own_ref[:, (HB - 1) * plane_cells + at].reshape(slots, c1)
                reg[HB + 1, y, z] = turned(at, 1)
                reg[HB + 2, y, z] = turned(plane_cells + at, 1)
            return carry

        lax.fori_loop(0, EDGE, load, 0)
        steps.masks(flags, emask, hmask, (0, 1, 2))
        weights[0].wait()

        def both(i, carry):
            steps.raise_cells(reg, up_ref, emask, ext, i * (EP - 1), (0, 1))
            return carry

        lax.fori_loop(0, 2, both, 0)
        steps.raise_cells(reg, up_ref, emask, ext, HB, (1,))
        for copy in copies:
            copy.wait()

        weights[1].wait()

        def hide(i, carry):
            x = jnp.where(i < INNER_H[0], i, i + INNER_H[1] - INNER_H[0])
            steps.hide(ext, first_ref, hmask, hid, x)
            return carry

        lax.fori_loop(0, HEDGE - INNER_H[1] + INNER_H[0], hide, 0)

        weights[2].wait()

        def refine(i, carry):
            x = jnp.where(i < low_o, i, i + INNER_O[1] - low_o)
            steps.refine(ext, hid, second_ref, rows, x, i)
            return carry

        lax.fori_loop(0, low_o + high_o, refine, 0)
        ends = [
            pltpu.make_async_copy(
                rows.at[:, pl.ds(0, low_o * plane)], out_ref.at[:, pl.ds(0, low_o * plane)],
                sem.at[8],
            ),
            pltpu.make_async_copy(
                rows.at[:, pl.ds(low_o * plane, high_o * plane)],
                out_ref.at[:, pl.ds(INNER_O[1] * plane, high_o * plane)],
                sem.at[9],
            ),
        ]
        for copy in ends:
            copy.start()
        for copy in ends:
            copy.wait()

    return pl.pallas_call(
        kernel,
        in_specs=[VMEM] * 2 + [HBM] * 6,
        out_specs=HBM,
        out_shape=jax.ShapeDtypeStruct((slots, BE * plane), jnp.bfloat16),
        scratch_shapes=steps.scratch()
        + [
            pltpu.VMEM((slots, (low_o + high_o) * plane), jnp.bfloat16),
            pltpu.SemaphoreType.DMA((10,)),
        ],
        input_output_aliases={7: 0},
        compiler_params=pltpu.CompilerParams(vmem_limit_bytes=64_000_000),
        cost_estimate=cost(8_000_000_000, 6_000_000),
    )(own, rims, up_pairs, first_pairs, second_pairs, ext_kept, hid_kept, out)


def to_owners(array):
    return lax.all_to_all(array, "grp", split_axis=0, concat_axis=0, tiled=True)


def local(latents, up_weight, first_weight, second_weight, brick_ids, brick_owner, neighbor_live):
    group = lax.axis_size("grp")
    capacity = max(2, brick_ids.shape[0] // group)
    assert latents.shape[0] == HB
    own, told = gather_own(
        latents, brick_ids, brick_owner, neighbor_live, group, capacity
    )
    own = to_owners(own)
    heard = to_owners(told)
    rims = gather_rims(latents, heard, group, capacity)
    rims = to_owners(rims)
    pairs = pair_weights(up_weight, first_weight, second_weight, heard)
    out, ext_kept, hid_kept = decode_inner(own, *pairs)
    return decode_outer(own, rims, out, ext_kept, hid_kept, *pairs)


def solution(mesh):
    in_specs = (
        P(("shape", "grp"), None, None, None),
        P(),
        P(),
        P(),
        P(("shape", "grp")),
        P(("shape", "grp")),
        P(("shape", "grp"), None),
    )
    out_specs = P(("shape", "grp"), None)
    return jax.shard_map(local, mesh=mesh, in_specs=in_specs, out_specs=out_specs, check_vma=False)
```

```python
import jax
import jax.numpy as jnp
from jax import lax
from jax.experimental import pallas as pl
from jax.experimental.pallas import tpu as pltpu
from jax.sharding import PartitionSpec as P


BE = 8
HB = 4
EDGE = HB + 3
WIN = 16
FAR = -1000
BIG = 65_536_000
WEIGHT_ROWS = 36_864

EEDGE = BE + 4
HEDGE = BE + 2
EP = EEDGE // 2
HP = HEDGE // 2
OP = BE // 2

taps = (((1, 0),), ((2, 0), (0, 1)))

VMEM = pl.BlockSpec(memory_space=pltpu.VMEM)
SMEM = pl.BlockSpec(memory_space=pltpu.SMEM)
HBM = pl.BlockSpec(memory_space=pltpu.HBM)


def cost(flops, moved):
    return pl.CostEstimate(flops=flops, bytes_accessed=moved, transcendentals=0)


def parts(value, size):
    if size & (size - 1):
        return lax.div(value, size), lax.rem(value, size)
    return value >> (size.bit_length() - 1), value & (size - 1)


def brick_place(brick, across):
    rest, along_z = parts(jnp.maximum(brick, 0), across)
    return parts(rest, across)[1], along_z


def window_of(brick, grid):
    across = grid // HB
    along_y, along_z = brick_place(brick, across)
    low_y = along_y * HB - 1
    low_z = along_z * HB - 1
    start_y = jnp.clip(low_y, 0, grid - EDGE)
    start_z = jnp.clip(((low_z + 8) & -8) - 8, 0, grid - WIN)
    return start_y, low_y - start_y, start_z, low_z - start_z, along_y == across - 1


def spread(values, group_of, blank):
    row = jnp.full(group_of.shape, blank, jnp.int32)
    for entry, value in enumerate(values):
        row = jnp.where(group_of == entry, value, row)
    return row


def slot_targets(bricks, owners, capacity, group_of):
    owners = [jnp.where(brick >= 0, owner, -1) for brick, owner in zip(bricks, owners)]
    owner_row = spread(owners, group_of, -1)
    rank = jnp.zeros_like(owner_row)
    for entry, owner in enumerate(owners):
        rank += jnp.where((group_of > entry) & (owner_row == owner), 1, 0)
    return jnp.where(owner_row >= 0, owner_row * capacity + rank, -1)


def cut_windows(bricks, owners, latents_ref, plane, count, win, sem, pick, out_ref, base):
    grid = latents_ref.shape[1]
    channels = latents_ref.shape[3]
    listed = len(bricks)
    group, _, capacity, _ = out_ref.shape
    slots = group * capacity
    places = [window_of(brick, grid) for brick in bricks]
    copies = []
    for entry, (start_y, _, start_z, _, _) in enumerate(places):
        copy = pltpu.make_async_copy(
            latents_ref.at[
                pl.ds(plane, count),
                pl.ds(start_y, EDGE),
                pl.ds(pl.multiple_of(start_z, 8), WIN),
                :,
            ],
            win.at[entry],
            sem.at[entry],
        )
        copy.start()
        copies.append(copy)
    column = lax.broadcasted_iota(jnp.int32, (1, listed * WIN), 1)
    group_of, cell = parts(column, WIN)
    target = slot_targets(bricks, owners, capacity, group_of)

    def finish():
        shape = (EDGE * slots, listed * WIN)
        shift = spread([place[3] for place in places], group_of, FAR)
        late = spread([jnp.where(place[4], FAR, place[3]) for place in places], group_of, FAR)
        step, at = parts(lax.broadcasted_iota(jnp.int32, shape, 0), slots)
        same = at == target
        pick[0] = jnp.where(same & (step == cell - shift), 1.0, 0.0).astype(jnp.bfloat16)
        pick[1] = jnp.where(same & (step == cell - late), 1.0, 0.0).astype(jnp.bfloat16)
        for copy in copies:
            copy.wait()

        def line(y, carry):
            rows = [jnp.clip(y + place[1], 0, EDGE - 1) for place in places]
            planes = [
                jnp.concatenate([win[entry, x, rows[entry]] for entry in range(listed)], axis=0)
                for x in range(count)
            ]
            cut = jnp.dot(
                pick[(y >= EDGE - 2).astype(jnp.int32)],
                jnp.concatenate(planes, axis=1),
                preferred_element_type=jnp.float32,
            ).astype(jnp.bfloat16)
            for x in range(count):
                for z in range(EDGE):
                    out_ref[:, base + (x * EDGE + y) * EDGE + z] = cut[
                        z * slots : (z + 1) * slots, x * channels : (x + 1) * channels
                    ].reshape(group, capacity, channels)
            return carry

        lax.fori_loop(0, EDGE, line, 0, unroll=True)

    return target, cell, finish


def gather_own(latents, brick_ids, brick_owner, neighbor_live, group, capacity):
    grid = latents.shape[1]
    channels = latents.shape[3]
    across = grid // HB
    listed = brick_ids.shape[0]
    slots = group * capacity
    cells = HB * EDGE * EDGE

    def kernel(ids_ref, owner_ref, near_ref, latents_ref, out_ref, flags, win, pick, sem):
        me = lax.axis_index("grp")
        bricks = [ids_ref[entry] for entry in range(listed)]
        owners = [owner_ref[entry] for entry in range(listed)]
        target, cell, finish = cut_windows(
            bricks, owners, latents_ref, 0, HB, win, sem, pick, out_ref, 0
        )
        offset = lax.broadcasted_iota(jnp.int32, (1, 27), 1)
        step_x = offset // 9 - 1
        step_y = offset // 3 % 3 - 1
        step_z = offset % 3 - 1
        inside_x = (me + step_x >= 0) & (me + step_x < group)
        flags[...] = jnp.zeros_like(flags)
        for entry in range(listed):
            along_y, along_z = brick_place(bricks[entry], across)
            near_y = along_y + step_y
            near_z = along_z + step_z
            inside = inside_x & (near_y >= 0) & (near_y < across)
            inside = inside & (near_z >= 0) & (near_z < across)
            chosen = (near_ref[entry : entry + 1, :] > 0) | (offset == 13)
            flags[entry * WIN : entry * WIN + 1, 0:27] = jnp.where(inside & chosen, 1.0, 0.0)
        at = lax.broadcasted_iota(jnp.int32, (slots, listed * WIN), 0)
        chosen = jnp.where((at == target) & (cell == 0), 1.0, 0.0).astype(jnp.bfloat16)
        slot_flags = jnp.dot(
            chosen, flags[...].astype(jnp.bfloat16), preferred_element_type=jnp.float32
        )
        out_ref[:, cells] = slot_flags.astype(jnp.bfloat16).reshape(group, capacity, channels)
        finish()

    return pl.pallas_call(
        kernel,
        in_specs=[SMEM, SMEM, VMEM, HBM],
        out_specs=VMEM,
        out_shape=jax.ShapeDtypeStruct((group, cells + 1, capacity, channels), jnp.bfloat16),
        scratch_shapes=[
            pltpu.VMEM((listed * WIN, channels), jnp.float32),
            pltpu.VMEM((listed, HB, EDGE, WIN, channels), jnp.bfloat16),
            pltpu.VMEM((2, EDGE * slots, listed * WIN), jnp.bfloat16),
            pltpu.SemaphoreType.DMA((listed,)),
        ],
        compiler_params=pltpu.CompilerParams(vmem_limit_bytes=BIG),
        cost_estimate=cost(1_000_000_000, 3_000_000),
    )(brick_ids, brick_owner, neighbor_live, latents)


def gather_rims(latents, heard, listed, group, capacity):
    channels = latents.shape[3]
    slots = group * capacity
    plane_cells = EDGE * EDGE

    def kernel(heard_ref, latents_ref, out_ref, win_b, win_a, pick_b, pick_a, sem):
        me = lax.axis_index("grp")

        def lists_of(device, near):
            bricks = [
                jnp.where(near, heard_ref[device, 0, entry], -1) for entry in range(listed)
            ]
            return bricks, [heard_ref[device, 0, listed + entry] for entry in range(listed)]

        before = lists_of(jnp.where(me > 0, me - 1, group - 1), me > 0)
        after = lists_of(jnp.where(me < group - 1, me + 1, 0), me < group - 1)
        finish_b = cut_windows(*before, latents_ref, 0, 2, win_b, sem.at[0], pick_b, out_ref, 0)[2]
        finish_a = cut_windows(
            *after, latents_ref, HB - 1, 1, win_a, sem.at[1], pick_a, out_ref, 2 * plane_cells
        )[2]
        finish_b()
        finish_a()

    return pl.pallas_call(
        kernel,
        in_specs=[SMEM, HBM],
        out_specs=VMEM,
        out_shape=jax.ShapeDtypeStruct(
            (group, 3 * plane_cells, capacity, channels), jnp.bfloat16
        ),
        scratch_shapes=[
            pltpu.VMEM((listed, 2, EDGE, WIN, channels), jnp.bfloat16),
            pltpu.VMEM((listed, 1, EDGE, WIN, channels), jnp.bfloat16),
            pltpu.VMEM((2, EDGE * slots, listed * WIN), jnp.bfloat16),
            pltpu.VMEM((2, EDGE * slots, listed * WIN), jnp.bfloat16),
            pltpu.SemaphoreType.DMA((2, listed)),
        ],
        compiler_params=pltpu.CompilerParams(vmem_limit_bytes=BIG),
        cost_estimate=cost(1_000_000_000, 3_000_000),
    )(heard, latents)


def weight_moves(parts_of, packed, sem, inward):
    moves = []
    start = 0
    for i, part in enumerate(parts_of):
        rows = packed.at[pl.ds(start, part.shape[0])]
        source, target = (rows, part) if inward else (part, rows)
        moves.append(pltpu.make_async_copy(source, target, sem.at[i]))
        start += part.shape[0]
    return moves


def pair_weights(up_weight, first_weight, second_weight, after):
    c1, c2 = up_weight.shape[3:]
    quad = 4 * c2
    lookup = {(parity, shift): tap for parity in (0, 1) for tap, shift in taps[parity]}

    def kernel(up_ref, first_ref, second_ref, after_ref, packed, up_out, first_out, second_out,
               sem):
        moves = weight_moves((up_out, first_out, second_out), packed, sem, False)
        for kx in range(3):
            for dy in (0, 1):
                for dz in (0, 1):
                    for py in (0, 1):
                        both = []
                        for pz in (0, 1):
                            ty = lookup.get((py, dy))
                            tz = lookup.get((pz, dz))
                            both.append(
                                jnp.zeros((c2, c1), jnp.bfloat16)
                                if ty is None or tz is None
                                else up_ref[kx, ty, tz]
                            )
                        at = (dy * 2 + dz) * c1
                        up_out[kx * 4 * c1 + at : kx * 4 * c1 + at + c1, py * 2 * c2 : (py + 1) * 2 * c2] = (
                            jnp.concatenate(both, axis=0).T
                        )
        moves[0].start()
        for raw, out, move in (
            (first_ref, first_out, moves[1]),
            (second_ref, second_out, moves[2]),
        ):
            def tile(kx, carry, raw=raw, out=out):
                for dy in (0, 1):
                    for dz in (0, 1):
                        for iy in (0, 1):
                            for iz in (0, 1):
                                for oy in (0, 1):
                                    both = []
                                    for oz in (0, 1):
                                        ky = 2 * dy + iy - oy
                                        kz = 2 * dz + iz - oz
                                        both.append(
                                            raw[kx, ky, kz]
                                            if 0 <= ky <= 2 and 0 <= kz <= 2
                                            else jnp.zeros((c2, c2), jnp.bfloat16)
                                        )
                                    at = (dy * 2 + dz) * quad + (iy * 2 + iz) * c2
                                    at = pl.multiple_of(kx * 4 * quad + at, c2)
                                    out[pl.ds(at, c2), oy * 2 * c2 : (oy + 1) * 2 * c2] = (
                                        jnp.concatenate(both, axis=1)
                                    )
                return carry

            lax.fori_loop(0, 3, tile, 0)
            move.start()
        for move in moves:
            move.wait()

    shapes = ((12 * c1, quad), (12 * quad, quad), (12 * quad, quad))
    assert sum(shape[0] for shape in shapes) <= WEIGHT_ROWS
    return pl.pallas_call(
        kernel,
        in_specs=[VMEM, VMEM, VMEM, HBM],
        out_specs=HBM,
        out_shape=jax.ShapeDtypeStruct((WEIGHT_ROWS, quad), jnp.bfloat16),
        scratch_shapes=[pltpu.VMEM(shape, jnp.bfloat16) for shape in shapes]
        + [pltpu.SemaphoreType.DMA((3,))],
        compiler_params=pltpu.CompilerParams(vmem_limit_bytes=BIG),
        cost_estimate=cost(1_000_000_000, 6_000_000),
    )(jnp.swapaxes(up_weight, 3, 4), first_weight, second_weight, after)


def pair_class(p):
    return 0 if p == 0 else 2 if p == EP - 1 else 1


def cell_class(h):
    return 0 if h == 0 else 2 if h == HEDGE - 1 else 1


class Decoder:
    def __init__(self, slots, c1, quad):
        self.slots, self.c1, self.quad = slots, c1, quad

    def scratch(self):
        slots, quad = self.slots, self.quad
        return [
            pltpu.VMEM((EDGE, EDGE, EDGE, slots, self.c1), jnp.bfloat16),
            pltpu.VMEM((EEDGE, EP, EP, slots, quad), jnp.bfloat16),
            pltpu.VMEM((HEDGE, HP, HP, slots, quad), jnp.bfloat16),
            pltpu.VMEM((3, EP, EP, slots, quad // 2), jnp.bfloat16),
            pltpu.VMEM((3, HP, HP, slots, quad), jnp.bfloat16),
            pltpu.VMEM((slots, self.c1), jnp.float32),
            pltpu.VMEM((12 * self.c1, quad), jnp.bfloat16),
            pltpu.VMEM((12 * quad, quad), jnp.bfloat16),
            pltpu.VMEM((12 * quad, quad), jnp.bfloat16),
            pltpu.SemaphoreType.DMA((3,)),
        ]

    def masks(self, flags, emask, hmask, classes):
        half, c2 = self.quad // 2, self.quad // 4
        wide = {
            cx * 9 + n: jnp.broadcast_to(flags[:, cx * 9 + n : cx * 9 + n + 1], (self.slots, half))
            for cx in classes
            for n in range(9)
        }
        left = lax.broadcasted_iota(jnp.int32, (self.slots, half), 1) < c2
        for cx in classes:
            for py in range(EP):
                for pz in range(EP):
                    n = cx * 9 + pair_class(py) * 3 + pair_class(pz)
                    emask[cx, py, pz] = wide[n].astype(jnp.bfloat16)
            mixed = {}
            for py in range(HP):
                for pz in range(HP):
                    for ty in (0, 1):
                        n = cx * 9 + cell_class(2 * py + ty) * 3
                        key = (n + cell_class(2 * pz), n + cell_class(2 * pz + 1))
                        if key not in mixed:
                            mixed[key] = jnp.where(left, wide[key[0]], wide[key[1]]).astype(
                                jnp.bfloat16
                            )
                        hmask[cx, py, pz, :, ty * half : (ty + 1) * half] = mixed[key]

    def patch(self, reg, x):
        return jnp.concatenate(
            [
                reg[x, dy : dy + EP, dz : dz + EP].reshape(-1, self.c1)
                for dy in (0, 1)
                for dz in (0, 1)
            ],
            axis=1,
        )

    def raise_cells(self, reg, up_ref, emask, ext, px, parities):
        cx = jnp.where(px == 0, 0, jnp.where(px == EP - 1, 2, 1))
        mask = emask[cx].reshape(-1, self.quad // 2)
        mask = jnp.concatenate([mask, mask], axis=1)
        shape = (EP, EP, self.slots, self.quad)
        near = self.patch(reg, px)
        depth = 4 * self.c1
        if 0 in parities:
            even = jnp.dot(near, up_ref[depth : 2 * depth], preferred_element_type=jnp.float32)
            ext[2 * px] = (even.astype(jnp.bfloat16) * mask).reshape(shape)
        if 1 in parities:
            odd = jnp.dot(near, up_ref[2 * depth : 3 * depth], preferred_element_type=jnp.float32)
            odd += jnp.dot(self.patch(reg, px + 1), up_ref[0:depth], preferred_element_type=jnp.float32)
            ext[2 * px + 1] = (odd.astype(jnp.bfloat16) * mask).reshape(shape)

    def conv(self, source, x, pairs, weight_ref):
        pieces = [
            source[x + kx, dy : dy + pairs, dz : dz + pairs].reshape(-1, self.quad)
            for kx in range(3)
            for dy in (0, 1)
            for dz in (0, 1)
        ]
        return jnp.dot(
            jnp.concatenate(pieces, axis=1), weight_ref[...], preferred_element_type=jnp.float32
        )

    def hide(self, ext, first_ref, hmask, hid, x):
        value = self.conv(ext, x, HP, first_ref)
        cx = jnp.where(x == 0, 0, jnp.where(x == HEDGE - 1, 2, 1))
        value = (value * (1.0 / (1.0 + jnp.exp(-value)))).astype(jnp.bfloat16)
        value = value * hmask[cx].reshape(-1, self.quad)
        hid[x] = value.reshape(HP, HP, self.slots, self.quad)

    def refine(self, ext, hid, second_ref, rows, x, at):
        half = self.quad // 2
        value = self.conv(hid, x, OP, second_ref)
        centre = ext[x + 2, 1 : 1 + OP, 1 : 1 + OP].reshape(-1, self.quad)
        value = (value + centre.astype(jnp.float32)).astype(jnp.bfloat16)
        value = value.reshape(OP, OP, self.slots, self.quad)
        for py in range(OP):
            for ty in (0, 1):
                line = jnp.concatenate(
                    [value[py, pz, :, ty * half : (ty + 1) * half] for pz in range(OP)], axis=1
                )
                start = pl.multiple_of(at * BE * OP * half + (2 * py + ty) * OP * half, 128)
                rows[:, pl.ds(start, OP * half)] = line


INNER_H, INNER_O = (2, 7), (2, 5)
KEPT_E = (2, 3, 7, 8)
KEPT_H = (2, 3, 5, 6)
KEPT_ROWS = 64


def decode_inner(own, pairs):
    group, _, capacity, c1 = own.shape
    quad = pairs.shape[1]
    slots = group * capacity
    plane = BE * BE * quad // 4
    steps = Decoder(slots, c1, quad)
    width = (INNER_O[1] - INNER_O[0]) * plane

    def kernel(own_ref, packed, out_ref, kept,
               reg, ext, hid, emask, hmask, flags, up_ref, first_ref, second_ref, wsem, rows, sem):
        weights = weight_moves((up_ref, first_ref, second_ref), packed, wsem, True)
        for move in weights:
            move.start()
        flags[...] = own_ref[:, HB * EDGE * EDGE].reshape(slots, c1).astype(jnp.float32)

        def load(y, carry):
            for x in range(HB):
                for z in range(EDGE):
                    reg[1 + x, y, z] = own_ref[:, (x * EDGE + y) * EDGE + z].reshape(slots, c1)
            return carry

        lax.fori_loop(0, EDGE, load, 0)
        steps.masks(flags, emask, hmask, (1,))
        weights[0].wait()

        def both(px, carry):
            steps.raise_cells(reg, up_ref, emask, ext, px, (0, 1))
            return carry

        lax.fori_loop(1, HB, both, 0)
        steps.raise_cells(reg, up_ref, emask, ext, HB, (0,))
        copies = [
            pltpu.make_async_copy(ext.at[e], kept.at[i], sem.at[i])
            for i, e in enumerate(KEPT_E)
        ]
        for copy in copies:
            copy.start()

        weights[1].wait()

        def hide(x, carry):
            steps.hide(ext, first_ref, hmask, hid, x)
            return carry

        lax.fori_loop(INNER_H[0], INNER_H[1], hide, 0)
        more = [
            pltpu.make_async_copy(
                hid.at[h], kept.at[4 + i, pl.ds(0, HP), pl.ds(0, HP)], sem.at[4 + i]
            )
            for i, h in enumerate(KEPT_H)
        ]
        for copy in more:
            copy.start()

        weights[2].wait()

        def refine(x, carry):
            steps.refine(ext, hid, second_ref, rows, x, x - INNER_O[0])
            return carry

        lax.fori_loop(INNER_O[0], INNER_O[1], refine, 0)
        last = pltpu.make_async_copy(
            rows, out_ref.at[:, pl.ds(INNER_O[0] * plane, width)], sem.at[8]
        )
        last.start()
        for copy in copies + more + [last]:
            copy.wait()

    return pl.pallas_call(
        kernel,
        in_specs=[VMEM, HBM],
        out_specs=[HBM] * 2,
        out_shape=[
            jax.ShapeDtypeStruct((slots, BE * plane), jnp.bfloat16),
            jax.ShapeDtypeStruct((KEPT_ROWS, EP, EP, slots, quad), jnp.bfloat16),
        ],
        scratch_shapes=steps.scratch()
        + [pltpu.VMEM((slots, width), jnp.bfloat16), pltpu.SemaphoreType.DMA((9,))],
        compiler_params=pltpu.CompilerParams(vmem_limit_bytes=50_000_000),
        cost_estimate=cost(8_000_000_000, 6_000_000),
    )(own, pairs)


def decode_outer(own, rims, out, kept, pairs):
    group, _, capacity, c1 = own.shape
    quad = pairs.shape[1]
    slots = group * capacity
    plane = BE * BE * quad // 4
    steps = Decoder(slots, c1, quad)
    plane_cells = EDGE * EDGE
    low_o = INNER_O[0]
    high_o = BE - INNER_O[1]

    def kernel(own_ref, rims_ref, packed, kept, out_in, out_ref,
               reg, ext, hid, emask, hmask, flags, up_ref, first_ref, second_ref, wsem, rows, sem):
        weights = weight_moves((up_ref, first_ref, second_ref), packed, wsem, True)
        for move in weights:
            move.start()
        copies = [
            pltpu.make_async_copy(kept.at[i], ext.at[e], sem.at[i])
            for i, e in enumerate(KEPT_E)
        ] + [
            pltpu.make_async_copy(
                kept.at[4 + i, pl.ds(0, HP), pl.ds(0, HP)], hid.at[h], sem.at[4 + i]
            )
            for i, h in enumerate(KEPT_H)
        ]
        for copy in copies:
            copy.start()
        flags[...] = own_ref[:, HB * plane_cells].reshape(slots, c1).astype(jnp.float32)

        def turned(row, shift):
            value = rims_ref[:, row].reshape(slots, c1)
            cut = (shift % group) * capacity
            return jnp.concatenate([value[cut:], value[:cut]], axis=0)

        def load(y, carry):
            for z in range(EDGE):
                at = y * EDGE + z
                reg[0, y, z] = turned(2 * plane_cells + at, -1)
                reg[1, y, z] = own_ref[:, at].reshape(slots, c1)
                reg[HB, y, z] = own_ref[:, (HB - 1) * plane_cells + at].reshape(slots, c1)
                reg[HB + 1, y, z] = turned(at, 1)
                reg[HB + 2, y, z] = turned(plane_cells + at, 1)
            return carry

        lax.fori_loop(0, EDGE, load, 0)
        steps.masks(flags, emask, hmask, (0, 1, 2))
        weights[0].wait()

        def both(i, carry):
            steps.raise_cells(reg, up_ref, emask, ext, i * (EP - 1), (0, 1))
            return carry

        lax.fori_loop(0, 2, both, 0)
        steps.raise_cells(reg, up_ref, emask, ext, HB, (1,))
        for copy in copies:
            copy.wait()

        weights[1].wait()

        def hide(i, carry):
            x = jnp.where(i < INNER_H[0], i, i + INNER_H[1] - INNER_H[0])
            steps.hide(ext, first_ref, hmask, hid, x)
            return carry

        lax.fori_loop(0, HEDGE - INNER_H[1] + INNER_H[0], hide, 0)

        weights[2].wait()

        def refine(i, carry):
            x = jnp.where(i < low_o, i, i + INNER_O[1] - low_o)
            steps.refine(ext, hid, second_ref, rows, x, i)
            return carry

        lax.fori_loop(0, low_o + high_o, refine, 0)
        ends = [
            pltpu.make_async_copy(
                rows.at[:, pl.ds(0, low_o * plane)], out_ref.at[:, pl.ds(0, low_o * plane)],
                sem.at[8],
            ),
            pltpu.make_async_copy(
                rows.at[:, pl.ds(low_o * plane, high_o * plane)],
                out_ref.at[:, pl.ds(INNER_O[1] * plane, high_o * plane)],
                sem.at[9],
            ),
        ]
        for copy in ends:
            copy.start()
        for copy in ends:
            copy.wait()

    return pl.pallas_call(
        kernel,
        in_specs=[VMEM] * 2 + [HBM] * 3,
        out_specs=HBM,
        out_shape=jax.ShapeDtypeStruct((slots, BE * plane), jnp.bfloat16),
        scratch_shapes=steps.scratch()
        + [
            pltpu.VMEM((slots, (low_o + high_o) * plane), jnp.bfloat16),
            pltpu.SemaphoreType.DMA((10,)),
        ],
        input_output_aliases={4: 0},
        compiler_params=pltpu.CompilerParams(vmem_limit_bytes=50_000_000),
        cost_estimate=cost(8_000_000_000, 6_000_000),
    )(own, rims, pairs, kept, out)


def to_owners(array):
    return lax.all_to_all(array, "grp", split_axis=0, concat_axis=0, tiled=True)


def local(latents, up_weight, first_weight, second_weight, brick_ids, brick_owner, neighbor_live):
    group = lax.axis_size("grp")
    listed = brick_ids.shape[0]
    capacity = max(2, listed // group)
    assert latents.shape[0] == HB
    shape = (group, 1, listed)
    lists = [jnp.broadcast_to(each, shape) for each in (brick_ids, brick_owner)]
    heard = to_owners(jnp.concatenate(lists, axis=2))
    own = gather_own(latents, brick_ids, brick_owner, neighbor_live, group, capacity)
    own = to_owners(own)
    rims = gather_rims(latents, heard, listed, group, capacity)
    rims = to_owners(rims)
    pairs = pair_weights(up_weight, first_weight, second_weight, heard)
    out, kept = decode_inner(own, pairs)
    return decode_outer(own, rims, out, kept, pairs)


def solution(mesh):
    in_specs = (
        P(("shape", "grp"), None, None, None),
        P(),
        P(),
        P(),
        P(("shape", "grp")),
        P(("shape", "grp")),
        P(("shape", "grp"), None),
    )
    out_specs = P(("shape", "grp"), None)
    return jax.shard_map(local, mesh=mesh, in_specs=in_specs, out_specs=out_specs, check_vma=False)
```

```python
import jax
import jax.numpy as jnp
from jax import lax
from jax.experimental import pallas as pl
from jax.experimental.pallas import tpu as pltpu
from jax.sharding import PartitionSpec as P


BE = 8
HB = 4
EDGE = HB + 3
WIN = 16
FAR = -1000
BIG = 65_536_000
WEIGHT_ROWS = 36_864
INNER_ROWS = (320, 512, 512)
OUTER_ROWS = (320, 512, 400)

EEDGE = BE + 4
HEDGE = BE + 2
EP = EEDGE // 2
HP = HEDGE // 2
OP = BE // 2

taps = (((1, 0),), ((2, 0), (0, 1)))

VMEM = pl.BlockSpec(memory_space=pltpu.VMEM)
SMEM = pl.BlockSpec(memory_space=pltpu.SMEM)
HBM = pl.BlockSpec(memory_space=pltpu.HBM)


def cost(flops, moved):
    return pl.CostEstimate(flops=flops, bytes_accessed=moved, transcendentals=0)


def parts(value, size):
    if size & (size - 1):
        return lax.div(value, size), lax.rem(value, size)
    return value >> (size.bit_length() - 1), value & (size - 1)


def brick_place(brick, across):
    rest, along_z = parts(jnp.maximum(brick, 0), across)
    return parts(rest, across)[1], along_z


def window_of(brick, grid):
    across = grid // HB
    along_y, along_z = brick_place(brick, across)
    low_y = along_y * HB - 1
    low_z = along_z * HB - 1
    start_y = jnp.clip(low_y, 0, grid - EDGE)
    start_z = jnp.clip(((low_z + 8) & -8) - 8, 0, grid - WIN)
    return start_y, low_y - start_y, start_z, low_z - start_z, along_y == across - 1


def spread(values, group_of, blank):
    row = jnp.full(group_of.shape, blank, jnp.int32)
    for entry, value in enumerate(values):
        row = jnp.where(group_of == entry, value, row)
    return row


def slot_targets(bricks, owners, capacity, group_of):
    owners = [jnp.where(brick >= 0, owner, -1) for brick, owner in zip(bricks, owners)]
    owner_row = spread(owners, group_of, -1)
    rank = jnp.zeros_like(owner_row)
    for entry, owner in enumerate(owners):
        rank += jnp.where((group_of > entry) & (owner_row == owner), 1, 0)
    return jnp.where(owner_row >= 0, owner_row * capacity + rank, -1)


def cut_windows(bricks, owners, latents_ref, plane, count, win, sem, pick, out_ref, base):
    grid = latents_ref.shape[1]
    channels = latents_ref.shape[3]
    listed = len(bricks)
    group, _, capacity, _ = out_ref.shape
    slots = group * capacity
    places = [window_of(brick, grid) for brick in bricks]
    copies = []
    for entry, (start_y, _, start_z, _, _) in enumerate(places):
        copy = pltpu.make_async_copy(
            latents_ref.at[
                pl.ds(plane, count),
                pl.ds(start_y, EDGE),
                pl.ds(pl.multiple_of(start_z, 8), WIN),
                :,
            ],
            win.at[entry],
            sem.at[entry],
        )
        copy.start()
        copies.append(copy)
    column = lax.broadcasted_iota(jnp.int32, (1, listed * WIN), 1)
    group_of, cell = parts(column, WIN)
    target = slot_targets(bricks, owners, capacity, group_of)

    def finish():
        shape = (EDGE * slots, listed * WIN)
        shift = spread([place[3] for place in places], group_of, FAR)
        late = spread([jnp.where(place[4], FAR, place[3]) for place in places], group_of, FAR)
        step, at = parts(lax.broadcasted_iota(jnp.int32, shape, 0), slots)
        same = at == target
        pick[0] = jnp.where(same & (step == cell - shift), 1.0, 0.0).astype(jnp.bfloat16)
        pick[1] = jnp.where(same & (step == cell - late), 1.0, 0.0).astype(jnp.bfloat16)
        for copy in copies:
            copy.wait()

        def line(y, carry):
            rows = [jnp.clip(y + place[1], 0, EDGE - 1) for place in places]
            planes = [
                jnp.concatenate([win[entry, x, rows[entry]] for entry in range(listed)], axis=0)
                for x in range(count)
            ]
            cut = jnp.dot(
                pick[(y >= EDGE - 2).astype(jnp.int32)],
                jnp.concatenate(planes, axis=1),
                preferred_element_type=jnp.float32,
            ).astype(jnp.bfloat16)
            for x in range(count):
                for z in range(EDGE):
                    out_ref[:, base + (x * EDGE + y) * EDGE + z] = cut[
                        z * slots : (z + 1) * slots, x * channels : (x + 1) * channels
                    ].reshape(group, capacity, channels)
            return carry

        lax.fori_loop(0, EDGE, line, 0, unroll=True)

    return target, cell, finish


def gather_own(latents, brick_ids, brick_owner, neighbor_live, group, capacity):
    grid = latents.shape[1]
    channels = latents.shape[3]
    across = grid // HB
    listed = brick_ids.shape[0]
    slots = group * capacity
    cells = HB * EDGE * EDGE

    def kernel(ids_ref, owner_ref, near_ref, latents_ref, out_ref, flags, win, pick, sem):
        me = lax.axis_index("grp")
        bricks = [ids_ref[entry] for entry in range(listed)]
        owners = [owner_ref[entry] for entry in range(listed)]
        target, cell, finish = cut_windows(
            bricks, owners, latents_ref, 0, HB, win, sem, pick, out_ref, 0
        )
        offset = lax.broadcasted_iota(jnp.int32, (1, 27), 1)
        step_x = offset // 9 - 1
        step_y = offset // 3 % 3 - 1
        step_z = offset % 3 - 1
        inside_x = (me + step_x >= 0) & (me + step_x < group)
        flags[...] = jnp.zeros_like(flags)
        for entry in range(listed):
            along_y, along_z = brick_place(bricks[entry], across)
            near_y = along_y + step_y
            near_z = along_z + step_z
            inside = inside_x & (near_y >= 0) & (near_y < across)
            inside = inside & (near_z >= 0) & (near_z < across)
            chosen = (near_ref[entry : entry + 1, :] > 0) | (offset == 13)
            flags[entry * WIN : entry * WIN + 1, 0:27] = jnp.where(inside & chosen, 1.0, 0.0)
        at = lax.broadcasted_iota(jnp.int32, (slots, listed * WIN), 0)
        chosen = jnp.where((at == target) & (cell == 0), 1.0, 0.0).astype(jnp.bfloat16)
        slot_flags = jnp.dot(
            chosen, flags[...].astype(jnp.bfloat16), preferred_element_type=jnp.float32
        )
        out_ref[:, cells] = slot_flags.astype(jnp.bfloat16).reshape(group, capacity, channels)
        finish()

    return pl.pallas_call(
        kernel,
        in_specs=[SMEM, SMEM, VMEM, HBM],
        out_specs=VMEM,
        out_shape=jax.ShapeDtypeStruct((group, cells + 1, capacity, channels), jnp.bfloat16),
        scratch_shapes=[
            pltpu.VMEM((listed * WIN, channels), jnp.float32),
            pltpu.VMEM((listed, HB, EDGE, WIN, channels), jnp.bfloat16),
            pltpu.VMEM((2, EDGE * slots, listed * WIN), jnp.bfloat16),
            pltpu.SemaphoreType.DMA((listed,)),
        ],
        compiler_params=pltpu.CompilerParams(vmem_limit_bytes=BIG),
        cost_estimate=cost(1_000_000_000, 3_000_000),
    )(brick_ids, brick_owner, neighbor_live, latents)


def gather_rims(latents, heard, listed, group, capacity):
    channels = latents.shape[3]
    slots = group * capacity
    plane_cells = EDGE * EDGE

    def kernel(heard_ref, latents_ref, out_ref, win_b, win_a, pick_b, pick_a, sem):
        me = lax.axis_index("grp")

        def lists_of(device, near):
            bricks = [
                jnp.where(near, heard_ref[device, 0, entry], -1) for entry in range(listed)
            ]
            return bricks, [heard_ref[device, 0, listed + entry] for entry in range(listed)]

        before = lists_of(jnp.where(me > 0, me - 1, group - 1), me > 0)
        after = lists_of(jnp.where(me < group - 1, me + 1, 0), me < group - 1)
        finish_b = cut_windows(*before, latents_ref, 0, 2, win_b, sem.at[0], pick_b, out_ref, 0)[2]
        finish_a = cut_windows(
            *after, latents_ref, HB - 1, 1, win_a, sem.at[1], pick_a, out_ref, 2 * plane_cells
        )[2]
        finish_b()
        finish_a()

    return pl.pallas_call(
        kernel,
        in_specs=[SMEM, HBM],
        out_specs=VMEM,
        out_shape=jax.ShapeDtypeStruct(
            (group, 3 * plane_cells, capacity, channels), jnp.bfloat16
        ),
        scratch_shapes=[
            pltpu.VMEM((listed, 2, EDGE, WIN, channels), jnp.bfloat16),
            pltpu.VMEM((listed, 1, EDGE, WIN, channels), jnp.bfloat16),
            pltpu.VMEM((2, EDGE * slots, listed * WIN), jnp.bfloat16),
            pltpu.VMEM((2, EDGE * slots, listed * WIN), jnp.bfloat16),
            pltpu.SemaphoreType.DMA((2, listed)),
        ],
        compiler_params=pltpu.CompilerParams(vmem_limit_bytes=BIG),
        cost_estimate=cost(1_000_000_000, 3_000_000),
    )(heard, latents)


def weight_moves(parts_of, packed, sem, inward):
    moves = []
    start = 0
    for i, part in enumerate(parts_of):
        rows = packed.at[pl.ds(start, part.shape[0])]
        source, target = (rows, part) if inward else (part, rows)
        moves.append(pltpu.make_async_copy(source, target, sem.at[i]))
        start += part.shape[0]
    return moves


def pair_weights(up_weight, first_weight, second_weight, after):
    c1, c2 = up_weight.shape[3:]
    quad = 4 * c2
    lookup = {(parity, shift): tap for parity in (0, 1) for tap, shift in taps[parity]}

    def kernel(up_ref, first_ref, second_ref, after_ref, packed, up_out, first_out, second_out,
               sem):
        moves = weight_moves((up_out, first_out, second_out), packed, sem, False)
        for kx in range(3):
            for dy in (0, 1):
                for dz in (0, 1):
                    for py in (0, 1):
                        both = []
                        for pz in (0, 1):
                            ty = lookup.get((py, dy))
                            tz = lookup.get((pz, dz))
                            both.append(
                                jnp.zeros((c2, c1), jnp.bfloat16)
                                if ty is None or tz is None
                                else up_ref[kx, ty, tz]
                            )
                        at = (dy * 2 + dz) * c1
                        up_out[kx * 4 * c1 + at : kx * 4 * c1 + at + c1, py * 2 * c2 : (py + 1) * 2 * c2] = (
                            jnp.concatenate(both, axis=0).T
                        )
        moves[0].start()
        for raw, out, move in (
            (first_ref, first_out, moves[1]),
            (second_ref, second_out, moves[2]),
        ):
            def tile(kx, carry, raw=raw, out=out):
                for dy in (0, 1):
                    for dz in (0, 1):
                        for iy in (0, 1):
                            for iz in (0, 1):
                                for oy in (0, 1):
                                    both = []
                                    for oz in (0, 1):
                                        ky = 2 * dy + iy - oy
                                        kz = 2 * dz + iz - oz
                                        both.append(
                                            raw[kx, ky, kz]
                                            if 0 <= ky <= 2 and 0 <= kz <= 2
                                            else jnp.zeros((c2, c2), jnp.bfloat16)
                                        )
                                    at = (dy * 2 + dz) * quad + (iy * 2 + iz) * c2
                                    at = pl.multiple_of(kx * 4 * quad + at, c2)
                                    out[pl.ds(at, c2), oy * 2 * c2 : (oy + 1) * 2 * c2] = (
                                        jnp.concatenate(both, axis=1)
                                    )
                return carry

            lax.fori_loop(0, 3, tile, 0)
            move.start()
        for move in moves:
            move.wait()

    shapes = ((12 * c1, quad), (12 * quad, quad), (12 * quad, quad))
    assert sum(shape[0] for shape in shapes) <= WEIGHT_ROWS
    return pl.pallas_call(
        kernel,
        in_specs=[VMEM, VMEM, VMEM, HBM],
        out_specs=HBM,
        out_shape=jax.ShapeDtypeStruct((WEIGHT_ROWS, quad), jnp.bfloat16),
        scratch_shapes=[pltpu.VMEM(shape, jnp.bfloat16) for shape in shapes]
        + [pltpu.SemaphoreType.DMA((3,))],
        compiler_params=pltpu.CompilerParams(vmem_limit_bytes=BIG),
        cost_estimate=cost(1_000_000_000, 6_000_000),
    )(jnp.swapaxes(up_weight, 3, 4), first_weight, second_weight, after)


def pair_class(p):
    return 0 if p == 0 else 2 if p == EP - 1 else 1


def cell_class(h):
    return 0 if h == 0 else 2 if h == HEDGE - 1 else 1


class Decoder:
    def __init__(self, slots, c1, quad, limits):
        self.slots, self.c1, self.quad, self.limits = slots, c1, quad, limits

    def scratch(self):
        slots, quad = self.slots, self.quad
        return [
            pltpu.VMEM((EDGE, EDGE, EDGE, slots, self.c1), jnp.bfloat16),
            pltpu.VMEM((EEDGE, EP, EP, slots, quad), jnp.bfloat16),
            pltpu.VMEM((HEDGE, HP, HP, slots, quad), jnp.bfloat16),
            pltpu.VMEM((3, EP, EP, slots, quad // 2), jnp.bfloat16),
            pltpu.VMEM((3, HP, HP, slots, quad), jnp.bfloat16),
            pltpu.VMEM((slots, self.c1), jnp.float32),
            pltpu.VMEM((12 * self.c1, quad), jnp.bfloat16),
            pltpu.VMEM((12 * quad, quad), jnp.bfloat16),
            pltpu.VMEM((12 * quad, quad), jnp.bfloat16),
            pltpu.SemaphoreType.DMA((3,)),
        ]

    def masks(self, flags, emask, hmask, classes):
        half, c2 = self.quad // 2, self.quad // 4
        wide = {
            cx * 9 + n: jnp.broadcast_to(flags[:, cx * 9 + n : cx * 9 + n + 1], (self.slots, half))
            for cx in classes
            for n in range(9)
        }
        left = lax.broadcasted_iota(jnp.int32, (self.slots, half), 1) < c2
        for cx in classes:
            for py in range(EP):
                for pz in range(EP):
                    n = cx * 9 + pair_class(py) * 3 + pair_class(pz)
                    emask[cx, py, pz] = wide[n].astype(jnp.bfloat16)
            mixed = {}
            for py in range(HP):
                for pz in range(HP):
                    for ty in (0, 1):
                        n = cx * 9 + cell_class(2 * py + ty) * 3
                        key = (n + cell_class(2 * pz), n + cell_class(2 * pz + 1))
                        if key not in mixed:
                            mixed[key] = jnp.where(left, wide[key[0]], wide[key[1]]).astype(
                                jnp.bfloat16
                            )
                        hmask[cx, py, pz, :, ty * half : (ty + 1) * half] = mixed[key]

    def raise_cells(self, reg, up_ref, emask, ext, edges):
        depth = 4 * self.c1
        for parity, shifts in ((0, ((1, 0),)), (1, ((2, 0), (0, 1)))):
            planes = [edge for edge in edges if edge % 2 == parity]
            weight = jnp.concatenate(
                [up_ref[tap * depth : (tap + 1) * depth] for tap, _ in shifts], axis=0
            )
            for blocks in self.chunks(planes, EP, 0):
                pieces = [
                    jnp.concatenate(
                        [reg[x // 2 + shift, y + dy, z + dz] for x, y, z in blocks], axis=0
                    )
                    for _, shift in shifts
                    for dy in (0, 1)
                    for dz in (0, 1)
                ]
                value = jnp.dot(
                    jnp.concatenate(pieces, axis=1), weight, preferred_element_type=jnp.float32
                ).astype(jnp.bfloat16)
                for i, (x, y, z) in enumerate(blocks):
                    mask = emask[pair_class(x // 2), y, z]
                    mask = jnp.concatenate([mask, mask], axis=1)
                    ext[x, y, z] = value[i * self.slots : (i + 1) * self.slots] * mask

    def conv(self, source, blocks, weight_ref):
        pieces = [
            jnp.concatenate([source[x + kx, y + dy, z + dz] for x, y, z in blocks], axis=0)
            for kx in range(3)
            for dy in (0, 1)
            for dz in (0, 1)
        ]
        return jnp.dot(
            jnp.concatenate(pieces, axis=1), weight_ref[...], preferred_element_type=jnp.float32
        )

    def chunks(self, planes, pairs, step):
        blocks = [(x, y, z) for x in planes for y in range(pairs) for z in range(pairs)]
        count = -(-len(blocks) * self.slots // self.limits[step])
        ends = [len(blocks) * i // count for i in range(count + 1)]
        return [blocks[start:end] for start, end in zip(ends, ends[1:])]

    def hide(self, ext, first_ref, hmask, hid, planes):
        for blocks in self.chunks(planes, HP, 1):
            value = self.conv(ext, blocks, first_ref)
            value = (value * (1.0 / (1.0 + jnp.exp(-value)))).astype(jnp.bfloat16)
            for i, (x, y, z) in enumerate(blocks):
                one = value[i * self.slots : (i + 1) * self.slots]
                hid[x, y, z] = one * hmask[cell_class(x), y, z]

    def refine(self, ext, hid, second_ref, rows, planes):
        half = self.quad // 2
        for blocks in self.chunks(planes, OP, 2):
            value = self.conv(hid, blocks, second_ref)
            for i, (x, y, z) in enumerate(blocks):
                one = value[i * self.slots : (i + 1) * self.slots]
                one = one + ext[x + 2, y + 1, z + 1].astype(jnp.float32)
                one = one.astype(jnp.bfloat16)
                for ty in (0, 1):
                    line = (planes.index(x) * BE + 2 * y + ty) * OP + z
                    rows[:, line * half : (line + 1) * half] = one[:, ty * half : (ty + 1) * half]


INNER_E, INNER_H, INNER_O = (2, 9), (2, 7), (2, 5)
KEPT_E = (2, 3, 7, 8)
KEPT_H = (2, 3, 5, 6)
KEPT_ROWS = 64


def decode_inner(own, pairs):
    group, _, capacity, c1 = own.shape
    quad = pairs.shape[1]
    slots = group * capacity
    plane = BE * BE * quad // 4
    steps = Decoder(slots, c1, quad, INNER_ROWS)
    width = (INNER_O[1] - INNER_O[0]) * plane

    def kernel(own_ref, packed, out_ref, kept,
               reg, ext, hid, emask, hmask, flags, up_ref, first_ref, second_ref, wsem, rows, sem):
        weights = weight_moves((up_ref, first_ref, second_ref), packed, wsem, True)
        for move in weights:
            move.start()
        flags[...] = own_ref[:, HB * EDGE * EDGE].reshape(slots, c1).astype(jnp.float32)

        def load(y, carry):
            for x in range(HB):
                for z in range(EDGE):
                    reg[1 + x, y, z] = own_ref[:, (x * EDGE + y) * EDGE + z].reshape(slots, c1)
            return carry

        lax.fori_loop(0, EDGE, load, 0)
        steps.masks(flags, emask, hmask, (1,))
        weights[0].wait()

        steps.raise_cells(reg, up_ref, emask, ext, list(range(*INNER_E)))
        copies = [
            pltpu.make_async_copy(ext.at[e], kept.at[i], sem.at[i])
            for i, e in enumerate(KEPT_E)
        ]
        for copy in copies:
            copy.start()

        weights[1].wait()

        steps.hide(ext, first_ref, hmask, hid, list(range(*INNER_H)))
        more = [
            pltpu.make_async_copy(
                hid.at[h], kept.at[4 + i, pl.ds(0, HP), pl.ds(0, HP)], sem.at[4 + i]
            )
            for i, h in enumerate(KEPT_H)
        ]
        for copy in more:
            copy.start()

        weights[2].wait()

        steps.refine(ext, hid, second_ref, rows, list(range(*INNER_O)))
        last = pltpu.make_async_copy(
            rows, out_ref.at[:, pl.ds(INNER_O[0] * plane, width)], sem.at[8]
        )
        last.start()
        for copy in copies + more + [last]:
            copy.wait()

    return pl.pallas_call(
        kernel,
        in_specs=[VMEM, HBM],
        out_specs=[HBM] * 2,
        out_shape=[
            jax.ShapeDtypeStruct((slots, BE * plane), jnp.bfloat16),
            jax.ShapeDtypeStruct((KEPT_ROWS, EP, EP, slots, quad), jnp.bfloat16),
        ],
        scratch_shapes=steps.scratch()
        + [pltpu.VMEM((slots, width), jnp.bfloat16), pltpu.SemaphoreType.DMA((9,))],
        compiler_params=pltpu.CompilerParams(vmem_limit_bytes=50_000_000),
        cost_estimate=cost(8_000_000_000, 6_000_000),
    )(own, pairs)


def decode_outer(own, rims, out, kept, pairs):
    group, _, capacity, c1 = own.shape
    quad = pairs.shape[1]
    slots = group * capacity
    plane = BE * BE * quad // 4
    steps = Decoder(slots, c1, quad, OUTER_ROWS)
    plane_cells = EDGE * EDGE
    low_o = INNER_O[0]
    high_o = BE - INNER_O[1]

    def kernel(own_ref, rims_ref, packed, kept, out_in, out_ref,
               reg, ext, hid, emask, hmask, flags, up_ref, first_ref, second_ref, wsem, rows, sem):
        weights = weight_moves((up_ref, first_ref, second_ref), packed, wsem, True)
        for move in weights:
            move.start()
        copies = [
            pltpu.make_async_copy(kept.at[i], ext.at[e], sem.at[i])
            for i, e in enumerate(KEPT_E)
        ] + [
            pltpu.make_async_copy(
                kept.at[4 + i, pl.ds(0, HP), pl.ds(0, HP)], hid.at[h], sem.at[4 + i]
            )
            for i, h in enumerate(KEPT_H)
        ]
        for copy in copies:
            copy.start()
        flags[...] = own_ref[:, HB * plane_cells].reshape(slots, c1).astype(jnp.float32)

        def turned(row, shift):
            value = rims_ref[:, row].reshape(slots, c1)
            cut = (shift % group) * capacity
            return jnp.concatenate([value[cut:], value[:cut]], axis=0)

        def load(y, carry):
            for z in range(EDGE):
                at = y * EDGE + z
                reg[0, y, z] = turned(2 * plane_cells + at, -1)
                reg[1, y, z] = own_ref[:, at].reshape(slots, c1)
                reg[HB, y, z] = own_ref[:, (HB - 1) * plane_cells + at].reshape(slots, c1)
                reg[HB + 1, y, z] = turned(at, 1)
                reg[HB + 2, y, z] = turned(plane_cells + at, 1)
            return carry

        lax.fori_loop(0, EDGE, load, 0)
        steps.masks(flags, emask, hmask, (0, 1, 2))
        weights[0].wait()

        steps.raise_cells(
            reg, up_ref, emask, ext, list(range(INNER_E[0])) + list(range(INNER_E[1], EEDGE))
        )
        for copy in copies:
            copy.wait()

        weights[1].wait()

        steps.hide(
            ext, first_ref, hmask, hid,
            list(range(INNER_H[0])) + list(range(INNER_H[1], HEDGE)),
        )
        weights[2].wait()

        steps.refine(
            ext, hid, second_ref, rows, list(range(low_o)) + list(range(INNER_O[1], BE))
        )
        ends = [
            pltpu.make_async_copy(
                rows.at[:, pl.ds(0, low_o * plane)], out_ref.at[:, pl.ds(0, low_o * plane)],
                sem.at[8],
            ),
            pltpu.make_async_copy(
                rows.at[:, pl.ds(low_o * plane, high_o * plane)],
                out_ref.at[:, pl.ds(INNER_O[1] * plane, high_o * plane)],
                sem.at[9],
            ),
        ]
        for copy in ends:
            copy.start()
        for copy in ends:
            copy.wait()

    return pl.pallas_call(
        kernel,
        in_specs=[VMEM] * 2 + [HBM] * 3,
        out_specs=HBM,
        out_shape=jax.ShapeDtypeStruct((slots, BE * plane), jnp.bfloat16),
        scratch_shapes=steps.scratch()
        + [
            pltpu.VMEM((slots, (low_o + high_o) * plane), jnp.bfloat16),
            pltpu.SemaphoreType.DMA((10,)),
        ],
        input_output_aliases={4: 0},
        compiler_params=pltpu.CompilerParams(vmem_limit_bytes=50_000_000),
        cost_estimate=cost(8_000_000_000, 6_000_000),
    )(own, rims, pairs, kept, out)


def to_owners(array):
    return lax.all_to_all(array, "grp", split_axis=0, concat_axis=0, tiled=True)


def local(latents, up_weight, first_weight, second_weight, brick_ids, brick_owner, neighbor_live):
    group = lax.axis_size("grp")
    listed = brick_ids.shape[0]
    capacity = max(2, listed // group)
    assert latents.shape[0] == HB
    shape = (group, 1, listed)
    lists = [jnp.broadcast_to(each, shape) for each in (brick_ids, brick_owner)]
    heard = to_owners(jnp.concatenate(lists, axis=2))
    own = gather_own(latents, brick_ids, brick_owner, neighbor_live, group, capacity)
    own = to_owners(own)
    rims = gather_rims(latents, heard, listed, group, capacity)
    rims = to_owners(rims)
    pairs = pair_weights(up_weight, first_weight, second_weight, heard)
    out, kept = decode_inner(own, pairs)
    return decode_outer(own, rims, out, kept, pairs)


def solution(mesh):
    in_specs = (
        P(("shape", "grp"), None, None, None),
        P(),
        P(),
        P(),
        P(("shape", "grp")),
        P(("shape", "grp")),
        P(("shape", "grp"), None),
    )
    out_specs = P(("shape", "grp"), None)
    return jax.shard_map(local, mesh=mesh, in_specs=in_specs, out_specs=out_specs, check_vma=False)
```

```python
import jax
import jax.numpy as jnp
from jax import lax
from jax.experimental import pallas as pl
from jax.experimental.pallas import tpu as pltpu
from jax.sharding import PartitionSpec as P


BE = 8
HB = 4
EDGE = HB + 3
WIN = 16
FAR = -1000
HALF = 65_536
BIG = 65_536_000
WEIGHT_ROWS = 36_864
INNER_ROWS = (320, 512, 512)
OUTER_ROWS = (320, 512, 400)

EEDGE = BE + 4
HEDGE = BE + 2
EP = EEDGE // 2
HP = HEDGE // 2
OP = BE // 2

taps = (((1, 0),), ((2, 0), (0, 1)))

VMEM = pl.BlockSpec(memory_space=pltpu.VMEM)
SMEM = pl.BlockSpec(memory_space=pltpu.SMEM)
HBM = pl.BlockSpec(memory_space=pltpu.HBM)


def cost(flops, moved):
    return pl.CostEstimate(flops=flops, bytes_accessed=moved, transcendentals=0)


def parts(value, size):
    if size & (size - 1):
        return lax.div(value, size), lax.rem(value, size)
    return value >> (size.bit_length() - 1), value & (size - 1)


def brick_place(brick, across):
    rest, along_z = parts(jnp.maximum(brick, 0), across)
    return parts(rest, across)[1], along_z


def window_of(brick, grid):
    across = grid // HB
    along_y, along_z = brick_place(brick, across)
    low_y = along_y * HB - 1
    low_z = along_z * HB - 1
    start_y = jnp.clip(low_y, 0, grid - EDGE)
    start_z = jnp.clip(((low_z + 8) & -8) - 8, 0, grid - WIN)
    return start_y, low_y - start_y, start_z, low_z - start_z, along_y == across - 1


def spread(values, group_of, blank):
    row = jnp.full(group_of.shape, blank, jnp.int32)
    for entry, value in enumerate(values):
        row = jnp.where(group_of == entry, value, row)
    return row


def slot_targets(bricks, owners, capacity, group_of):
    owners = [jnp.where(brick >= 0, owner, -1) for brick, owner in zip(bricks, owners)]
    owner_row = spread(owners, group_of, -1)
    rank = jnp.zeros_like(owner_row)
    for entry, owner in enumerate(owners):
        rank += jnp.where((group_of > entry) & (owner_row == owner), 1, 0)
    return jnp.where(owner_row >= 0, owner_row * capacity + rank, -1)


def cut_windows(bricks, owners, latents_ref, plane, count, win, sem, pick, out_ref, base):
    grid = latents_ref.shape[1]
    channels = latents_ref.shape[3]
    listed = len(bricks)
    group, _, capacity, _ = out_ref.shape
    slots = group * capacity
    places = [window_of(brick, grid) for brick in bricks]
    copies = []
    for entry, (start_y, _, start_z, _, _) in enumerate(places):
        copy = pltpu.make_async_copy(
            latents_ref.at[
                pl.ds(plane, count),
                pl.ds(start_y, EDGE),
                pl.ds(pl.multiple_of(start_z, 8), WIN),
                :,
            ],
            win.at[entry],
            sem.at[entry],
        )
        copy.start()
        copies.append(copy)
    column = lax.broadcasted_iota(jnp.int32, (1, listed * WIN), 1)
    group_of, cell = parts(column, WIN)
    target = slot_targets(bricks, owners, capacity, group_of)

    def finish():
        shape = (EDGE * slots, listed * WIN)
        shift = spread([place[3] for place in places], group_of, FAR)
        late = spread([jnp.where(place[4], FAR, place[3]) for place in places], group_of, FAR)
        step, at = parts(lax.broadcasted_iota(jnp.int32, shape, 0), slots)
        same = at == target
        pick[0] = jnp.where(same & (step == cell - shift), 1.0, 0.0).astype(jnp.bfloat16)
        pick[1] = jnp.where(same & (step == cell - late), 1.0, 0.0).astype(jnp.bfloat16)
        for copy in copies:
            copy.wait()

        def line(y, carry):
            rows = [jnp.clip(y + place[1], 0, EDGE - 1) for place in places]
            planes = [
                jnp.concatenate([win[entry, x, rows[entry]] for entry in range(listed)], axis=0)
                for x in range(count)
            ]
            cut = jnp.dot(
                pick[(y >= EDGE - 2).astype(jnp.int32)],
                jnp.concatenate(planes, axis=1),
                preferred_element_type=jnp.float32,
            ).astype(jnp.bfloat16)
            for x in range(count):
                for z in range(EDGE):
                    out_ref[:, base + (x * EDGE + y) * EDGE + z] = cut[
                        z * slots : (z + 1) * slots, x * channels : (x + 1) * channels
                    ].reshape(group, capacity, channels)
            return carry

        lax.fori_loop(0, EDGE, line, 0, unroll=True)

    return target, cell, finish


def gather_own(latents, brick_ids, brick_owner, neighbor_live, group, capacity):
    grid = latents.shape[1]
    channels = latents.shape[3]
    across = grid // HB
    listed = brick_ids.shape[0]
    slots = group * capacity
    cells = HB * EDGE * EDGE

    def kernel(ids_ref, owner_ref, near_ref, latents_ref, out_ref, flags, win, pick, sem):
        me = lax.axis_index("grp")
        bricks = [ids_ref[entry] for entry in range(listed)]
        owners = [owner_ref[entry] for entry in range(listed)]
        target, cell, finish = cut_windows(
            bricks, owners, latents_ref, 0, HB, win, sem, pick, out_ref, 0
        )
        offset = lax.broadcasted_iota(jnp.int32, (1, 27), 1)
        step_x = offset // 9 - 1
        step_y = offset // 3 % 3 - 1
        step_z = offset % 3 - 1
        inside_x = (me + step_x >= 0) & (me + step_x < group)
        flags[...] = jnp.zeros_like(flags)
        for entry in range(listed):
            along_y, along_z = brick_place(bricks[entry], across)
            near_y = along_y + step_y
            near_z = along_z + step_z
            inside = inside_x & (near_y >= 0) & (near_y < across)
            inside = inside & (near_z >= 0) & (near_z < across)
            chosen = (near_ref[entry : entry + 1, :] > 0) | (offset == 13)
            flags[entry * WIN : entry * WIN + 1, 0:27] = jnp.where(inside & chosen, 1.0, 0.0)
        at = lax.broadcasted_iota(jnp.int32, (slots, listed * WIN), 0)
        chosen = jnp.where((at == target) & (cell == 0), 1.0, 0.0).astype(jnp.bfloat16)
        slot_flags = jnp.dot(
            chosen, flags[...].astype(jnp.bfloat16), preferred_element_type=jnp.float32
        )
        out_ref[:, cells] = slot_flags.astype(jnp.bfloat16).reshape(group, capacity, channels)
        finish()

    return pl.pallas_call(
        kernel,
        in_specs=[SMEM, SMEM, VMEM, HBM],
        out_specs=VMEM,
        out_shape=jax.ShapeDtypeStruct((group, cells + 1, capacity, channels), jnp.bfloat16),
        scratch_shapes=[
            pltpu.VMEM((listed * WIN, channels), jnp.float32),
            pltpu.VMEM((listed, HB, EDGE, WIN, channels), jnp.bfloat16),
            pltpu.VMEM((2, EDGE * slots, listed * WIN), jnp.bfloat16),
            pltpu.SemaphoreType.DMA((listed,)),
        ],
        compiler_params=pltpu.CompilerParams(vmem_limit_bytes=BIG),
        cost_estimate=cost(1_000_000_000, 3_000_000),
    )(brick_ids, brick_owner, neighbor_live, latents)


def gather_rims(latents, heard, listed, group, capacity):
    channels = latents.shape[3]
    slots = group * capacity
    plane_cells = EDGE * EDGE

    def kernel(heard_ref, latents_ref, out_ref, win_b, win_a, pick_b, pick_a, sem):
        me = lax.axis_index("grp")

        def lists_of(device, near):
            both = [heard_ref[device, 0, entry] for entry in range(listed)]
            used = [near & (code >= 0) for code in both]
            halves = [parts(jnp.maximum(code, 0), HALF) for code in both]
            bricks = [jnp.where(use, half[0], -1) for use, half in zip(used, halves)]
            return bricks, [half[1] for half in halves]

        before = lists_of(jnp.where(me > 0, me - 1, group - 1), me > 0)
        after = lists_of(jnp.where(me < group - 1, me + 1, 0), me < group - 1)
        finish_b = cut_windows(*before, latents_ref, 0, 2, win_b, sem.at[0], pick_b, out_ref, 0)[2]
        finish_a = cut_windows(
            *after, latents_ref, HB - 1, 1, win_a, sem.at[1], pick_a, out_ref, 2 * plane_cells
        )[2]
        finish_b()
        finish_a()

    return pl.pallas_call(
        kernel,
        in_specs=[SMEM, HBM],
        out_specs=VMEM,
        out_shape=jax.ShapeDtypeStruct(
            (group, 3 * plane_cells, capacity, channels), jnp.bfloat16
        ),
        scratch_shapes=[
            pltpu.VMEM((listed, 2, EDGE, WIN, channels), jnp.bfloat16),
            pltpu.VMEM((listed, 1, EDGE, WIN, channels), jnp.bfloat16),
            pltpu.VMEM((2, EDGE * slots, listed * WIN), jnp.bfloat16),
            pltpu.VMEM((2, EDGE * slots, listed * WIN), jnp.bfloat16),
            pltpu.SemaphoreType.DMA((2, listed)),
        ],
        compiler_params=pltpu.CompilerParams(vmem_limit_bytes=BIG),
        cost_estimate=cost(1_000_000_000, 3_000_000),
    )(heard, latents)


def weight_moves(parts_of, packed, sem, inward):
    moves = []
    start = 0
    for i, part in enumerate(parts_of):
        rows = packed.at[pl.ds(start, part.shape[0])]
        source, target = (rows, part) if inward else (part, rows)
        moves.append(pltpu.make_async_copy(source, target, sem.at[i]))
        start += part.shape[0]
    return moves


def pair_weights(up_weight, first_weight, second_weight, after):
    c1, c2 = up_weight.shape[3:]
    quad = 4 * c2
    lookup = {(parity, shift): tap for parity in (0, 1) for tap, shift in taps[parity]}

    def kernel(up_ref, first_ref, second_ref, after_ref, packed, up_out, first_out, second_out,
               sem):
        moves = weight_moves((up_out, first_out, second_out), packed, sem, False)
        for kx in range(3):
            for dy in (0, 1):
                for dz in (0, 1):
                    for py in (0, 1):
                        both = []
                        for pz in (0, 1):
                            ty = lookup.get((py, dy))
                            tz = lookup.get((pz, dz))
                            both.append(
                                jnp.zeros((c2, c1), jnp.bfloat16)
                                if ty is None or tz is None
                                else up_ref[kx, ty, tz]
                            )
                        at = (dy * 2 + dz) * c1
                        up_out[kx * 4 * c1 + at : kx * 4 * c1 + at + c1, py * 2 * c2 : (py + 1) * 2 * c2] = (
                            jnp.concatenate(both, axis=0).T
                        )
        moves[0].start()
        for raw, out, move in (
            (first_ref, first_out, moves[1]),
            (second_ref, second_out, moves[2]),
        ):
            def tile(kx, carry, raw=raw, out=out):
                for dy in (0, 1):
                    for dz in (0, 1):
                        for iy in (0, 1):
                            for iz in (0, 1):
                                for oy in (0, 1):
                                    both = []
                                    for oz in (0, 1):
                                        ky = 2 * dy + iy - oy
                                        kz = 2 * dz + iz - oz
                                        both.append(
                                            raw[kx, ky, kz]
                                            if 0 <= ky <= 2 and 0 <= kz <= 2
                                            else jnp.zeros((c2, c2), jnp.bfloat16)
                                        )
                                    at = (dy * 2 + dz) * quad + (iy * 2 + iz) * c2
                                    at = pl.multiple_of(kx * 4 * quad + at, c2)
                                    out[pl.ds(at, c2), oy * 2 * c2 : (oy + 1) * 2 * c2] = (
                                        jnp.concatenate(both, axis=1)
                                    )
                return carry

            lax.fori_loop(0, 3, tile, 0)
            move.start()
        for move in moves:
            move.wait()

    shapes = ((12 * c1, quad), (12 * quad, quad), (12 * quad, quad))
    assert sum(shape[0] for shape in shapes) <= WEIGHT_ROWS
    return pl.pallas_call(
        kernel,
        in_specs=[VMEM, VMEM, VMEM, HBM],
        out_specs=HBM,
        out_shape=jax.ShapeDtypeStruct((WEIGHT_ROWS, quad), jnp.bfloat16),
        scratch_shapes=[pltpu.VMEM(shape, jnp.bfloat16) for shape in shapes]
        + [pltpu.SemaphoreType.DMA((3,))],
        compiler_params=pltpu.CompilerParams(vmem_limit_bytes=BIG),
        cost_estimate=cost(1_000_000_000, 6_000_000),
    )(jnp.swapaxes(up_weight, 3, 4), first_weight, second_weight, after)


def pair_class(p):
    return 0 if p == 0 else 2 if p == EP - 1 else 1


def cell_class(h):
    return 0 if h == 0 else 2 if h == HEDGE - 1 else 1


class Decoder:
    def __init__(self, slots, c1, quad, limits):
        self.slots, self.c1, self.quad, self.limits = slots, c1, quad, limits

    def scratch(self):
        slots, quad = self.slots, self.quad
        return [
            pltpu.VMEM((EDGE, EDGE, EDGE, slots, self.c1), jnp.bfloat16),
            pltpu.VMEM((EEDGE, EP, EP, slots, quad), jnp.bfloat16),
            pltpu.VMEM((HEDGE, HP, HP, slots, quad), jnp.bfloat16),
            pltpu.VMEM((3, EP, EP, slots, quad // 2), jnp.bfloat16),
            pltpu.VMEM((3, HP, HP, slots, quad), jnp.bfloat16),
            pltpu.VMEM((slots, self.c1), jnp.float32),
            pltpu.VMEM((12 * self.c1, quad), jnp.bfloat16),
            pltpu.VMEM((12 * quad, quad), jnp.bfloat16),
            pltpu.VMEM((12 * quad, quad), jnp.bfloat16),
            pltpu.SemaphoreType.DMA((3,)),
        ]

    def masks(self, flags, emask, hmask, classes):
        half, c2 = self.quad // 2, self.quad // 4
        wide = {
            cx * 9 + n: jnp.broadcast_to(flags[:, cx * 9 + n : cx * 9 + n + 1], (self.slots, half))
            for cx in classes
            for n in range(9)
        }
        left = lax.broadcasted_iota(jnp.int32, (self.slots, half), 1) < c2
        for cx in classes:
            for py in range(EP):
                for pz in range(EP):
                    n = cx * 9 + pair_class(py) * 3 + pair_class(pz)
                    emask[cx, py, pz] = wide[n].astype(jnp.bfloat16)
            mixed = {}
            for py in range(HP):
                for pz in range(HP):
                    for ty in (0, 1):
                        n = cx * 9 + cell_class(2 * py + ty) * 3
                        key = (n + cell_class(2 * pz), n + cell_class(2 * pz + 1))
                        if key not in mixed:
                            mixed[key] = jnp.where(left, wide[key[0]], wide[key[1]]).astype(
                                jnp.bfloat16
                            )
                        hmask[cx, py, pz, :, ty * half : (ty + 1) * half] = mixed[key]

    def raise_cells(self, reg, up_ref, emask, ext, edges):
        depth = 4 * self.c1
        for parity, shifts in ((0, ((1, 0),)), (1, ((2, 0), (0, 1)))):
            planes = [edge for edge in edges if edge % 2 == parity]
            weight = jnp.concatenate(
                [up_ref[tap * depth : (tap + 1) * depth] for tap, _ in shifts], axis=0
            )
            for blocks in self.chunks(planes, EP, 0):
                pieces = [
                    jnp.concatenate(
                        [reg[x // 2 + shift, y + dy, z + dz] for x, y, z in blocks], axis=0
                    )
                    for _, shift in shifts
                    for dy in (0, 1)
                    for dz in (0, 1)
                ]
                value = jnp.dot(
                    jnp.concatenate(pieces, axis=1), weight, preferred_element_type=jnp.float32
                ).astype(jnp.bfloat16)
                for i, (x, y, z) in enumerate(blocks):
                    mask = emask[pair_class(x // 2), y, z]
                    mask = jnp.concatenate([mask, mask], axis=1)
                    ext[x, y, z] = value[i * self.slots : (i + 1) * self.slots] * mask

    def conv(self, source, blocks, weight_ref):
        pieces = [
            jnp.concatenate([source[x + kx, y + dy, z + dz] for x, y, z in blocks], axis=0)
            for kx in range(3)
            for dy in (0, 1)
            for dz in (0, 1)
        ]
        return jnp.dot(
            jnp.concatenate(pieces, axis=1), weight_ref[...], preferred_element_type=jnp.float32
        )

    def chunks(self, planes, pairs, step):
        blocks = [(x, y, z) for x in planes for y in range(pairs) for z in range(pairs)]
        count = -(-len(blocks) * self.slots // self.limits[step])
        ends = [len(blocks) * i // count for i in range(count + 1)]
        return [blocks[start:end] for start, end in zip(ends, ends[1:])]

    def hide(self, ext, first_ref, hmask, hid, planes):
        for blocks in self.chunks(planes, HP, 1):
            value = self.conv(ext, blocks, first_ref)
            value = (value * (1.0 / (1.0 + jnp.exp(-value)))).astype(jnp.bfloat16)
            for i, (x, y, z) in enumerate(blocks):
                one = value[i * self.slots : (i + 1) * self.slots]
                hid[x, y, z] = one * hmask[cell_class(x), y, z]

    def refine(self, ext, hid, second_ref, rows, planes):
        half = self.quad // 2
        for blocks in self.chunks(planes, OP, 2):
            value = self.conv(hid, blocks, second_ref)
            for i, (x, y, z) in enumerate(blocks):
                one = value[i * self.slots : (i + 1) * self.slots]
                one = one + ext[x + 2, y + 1, z + 1].astype(jnp.float32)
                one = one.astype(jnp.bfloat16)
                for ty in (0, 1):
                    line = (planes.index(x) * BE + 2 * y + ty) * OP + z
                    rows[:, line * half : (line + 1) * half] = one[:, ty * half : (ty + 1) * half]


INNER_E, INNER_H, INNER_O = (2, 9), (2, 7), (2, 5)
KEPT_E = (2, 3, 7, 8)
KEPT_H = (2, 3, 5, 6)
KEPT_ROWS = 64


def decode_inner(own, pairs):
    group, _, capacity, c1 = own.shape
    quad = pairs.shape[1]
    slots = group * capacity
    plane = BE * BE * quad // 4
    steps = Decoder(slots, c1, quad, INNER_ROWS)
    width = (INNER_O[1] - INNER_O[0]) * plane

    def kernel(own_ref, packed, out_ref, kept,
               reg, ext, hid, emask, hmask, flags, up_ref, first_ref, second_ref, wsem, rows, sem):
        weights = weight_moves((up_ref, first_ref, second_ref), packed, wsem, True)
        for move in weights:
            move.start()
        flags[...] = own_ref[:, HB * EDGE * EDGE].reshape(slots, c1).astype(jnp.float32)

        def load(y, carry):
            for x in range(HB):
                for z in range(EDGE):
                    reg[1 + x, y, z] = own_ref[:, (x * EDGE + y) * EDGE + z].reshape(slots, c1)
            return carry

        lax.fori_loop(0, EDGE, load, 0, unroll=True)
        steps.masks(flags, emask, hmask, (1,))
        weights[0].wait()

        steps.raise_cells(reg, up_ref, emask, ext, list(range(*INNER_E)))
        copies = [
            pltpu.make_async_copy(ext.at[e], kept.at[i], sem.at[i])
            for i, e in enumerate(KEPT_E)
        ]
        for copy in copies:
            copy.start()

        weights[1].wait()

        steps.hide(ext, first_ref, hmask, hid, list(range(*INNER_H)))
        more = [
            pltpu.make_async_copy(
                hid.at[h], kept.at[4 + i, pl.ds(0, HP), pl.ds(0, HP)], sem.at[4 + i]
            )
            for i, h in enumerate(KEPT_H)
        ]
        for copy in more:
            copy.start()

        weights[2].wait()

        steps.refine(ext, hid, second_ref, rows, list(range(*INNER_O)))
        last = pltpu.make_async_copy(
            rows, out_ref.at[:, pl.ds(INNER_O[0] * plane, width)], sem.at[8]
        )
        last.start()
        for copy in copies + more + [last]:
            copy.wait()

    return pl.pallas_call(
        kernel,
        in_specs=[VMEM, HBM],
        out_specs=[HBM] * 2,
        out_shape=[
            jax.ShapeDtypeStruct((slots, BE * plane), jnp.bfloat16),
            jax.ShapeDtypeStruct((KEPT_ROWS, EP, EP, slots, quad), jnp.bfloat16),
        ],
        scratch_shapes=steps.scratch()
        + [pltpu.VMEM((slots, width), jnp.bfloat16), pltpu.SemaphoreType.DMA((9,))],
        compiler_params=pltpu.CompilerParams(vmem_limit_bytes=50_000_000),
        cost_estimate=cost(8_000_000_000, 6_000_000),
    )(own, pairs)


def decode_outer(own, rims, out, kept, pairs):
    group, _, capacity, c1 = own.shape
    quad = pairs.shape[1]
    slots = group * capacity
    plane = BE * BE * quad // 4
    steps = Decoder(slots, c1, quad, OUTER_ROWS)
    plane_cells = EDGE * EDGE
    low_o = INNER_O[0]
    high_o = BE - INNER_O[1]

    def kernel(own_ref, rims_ref, packed, kept, out_in, out_ref,
               reg, ext, hid, emask, hmask, flags, up_ref, first_ref, second_ref, wsem, rows, sem):
        weights = weight_moves((up_ref, first_ref, second_ref), packed, wsem, True)
        for move in weights:
            move.start()
        copies = [
            pltpu.make_async_copy(kept.at[i], ext.at[e], sem.at[i])
            for i, e in enumerate(KEPT_E)
        ] + [
            pltpu.make_async_copy(
                kept.at[4 + i, pl.ds(0, HP), pl.ds(0, HP)], hid.at[h], sem.at[4 + i]
            )
            for i, h in enumerate(KEPT_H)
        ]
        for copy in copies:
            copy.start()
        flags[...] = own_ref[:, HB * plane_cells].reshape(slots, c1).astype(jnp.float32)

        def turned(row, shift):
            value = rims_ref[:, row].reshape(slots, c1)
            cut = (shift % group) * capacity
            return jnp.concatenate([value[cut:], value[:cut]], axis=0)

        def load(y, carry):
            for z in range(EDGE):
                at = y * EDGE + z
                reg[0, y, z] = turned(2 * plane_cells + at, -1)
                reg[1, y, z] = own_ref[:, at].reshape(slots, c1)
                reg[HB, y, z] = own_ref[:, (HB - 1) * plane_cells + at].reshape(slots, c1)
                reg[HB + 1, y, z] = turned(at, 1)
                reg[HB + 2, y, z] = turned(plane_cells + at, 1)
            return carry

        lax.fori_loop(0, EDGE, load, 0, unroll=True)
        steps.masks(flags, emask, hmask, (0, 1, 2))
        weights[0].wait()

        steps.raise_cells(
            reg, up_ref, emask, ext, list(range(INNER_E[0])) + list(range(INNER_E[1], EEDGE))
        )
        for copy in copies:
            copy.wait()

        weights[1].wait()

        steps.hide(
            ext, first_ref, hmask, hid,
            list(range(INNER_H[0])) + list(range(INNER_H[1], HEDGE)),
        )
        weights[2].wait()

        steps.refine(
            ext, hid, second_ref, rows, list(range(low_o)) + list(range(INNER_O[1], BE))
        )
        ends = [
            pltpu.make_async_copy(
                rows.at[:, pl.ds(0, low_o * plane)], out_ref.at[:, pl.ds(0, low_o * plane)],
                sem.at[8],
            ),
            pltpu.make_async_copy(
                rows.at[:, pl.ds(low_o * plane, high_o * plane)],
                out_ref.at[:, pl.ds(INNER_O[1] * plane, high_o * plane)],
                sem.at[9],
            ),
        ]
        for copy in ends:
            copy.start()
        for copy in ends:
            copy.wait()

    return pl.pallas_call(
        kernel,
        in_specs=[VMEM] * 2 + [HBM] * 3,
        out_specs=HBM,
        out_shape=jax.ShapeDtypeStruct((slots, BE * plane), jnp.bfloat16),
        scratch_shapes=steps.scratch()
        + [
            pltpu.VMEM((slots, (low_o + high_o) * plane), jnp.bfloat16),
            pltpu.SemaphoreType.DMA((10,)),
        ],
        input_output_aliases={4: 0},
        compiler_params=pltpu.CompilerParams(vmem_limit_bytes=50_000_000),
        cost_estimate=cost(8_000_000_000, 6_000_000),
    )(own, rims, pairs, kept, out)


def to_owners(array):
    return lax.all_to_all(array, "grp", split_axis=0, concat_axis=0, tiled=True)


def local(latents, up_weight, first_weight, second_weight, brick_ids, brick_owner, neighbor_live):
    group = lax.axis_size("grp")
    listed = brick_ids.shape[0]
    capacity = max(2, listed // group)
    assert latents.shape[0] == HB
    both = jnp.where(brick_ids >= 0, brick_ids * HALF + brick_owner, -1)
    heard = to_owners(jnp.broadcast_to(both, (group, 1, listed)))
    own = gather_own(latents, brick_ids, brick_owner, neighbor_live, group, capacity)
    own = to_owners(own)
    rims = gather_rims(latents, heard, listed, group, capacity)
    rims = to_owners(rims)
    pairs = pair_weights(up_weight, first_weight, second_weight, heard)
    out, kept = decode_inner(own, pairs)
    return decode_outer(own, rims, out, kept, pairs)


def solution(mesh):
    in_specs = (
        P(("shape", "grp"), None, None, None),
        P(),
        P(),
        P(),
        P(("shape", "grp")),
        P(("shape", "grp")),
        P(("shape", "grp"), None),
    )
    out_specs = P(("shape", "grp"), None)
    return jax.shard_map(local, mesh=mesh, in_specs=in_specs, out_specs=out_specs, check_vma=False)
```

```python
import jax
import jax.numpy as jnp
from jax import lax
from jax.experimental import pallas as pl
from jax.experimental.pallas import tpu as pltpu
from jax.sharding import PartitionSpec as P


BE = 8
HB = 4
EDGE = HB + 3
WIN = 16
FAR = -1000
HALF = 65_536
BIG = 65_536_000
WEIGHT_ROWS = 36_864
INNER_ROWS = (320, 512, 512)
OUTER_ROWS = (320, 512, 400)

EEDGE = BE + 4
HEDGE = BE + 2
EP = EEDGE // 2
HP = HEDGE // 2
OP = BE // 2

taps = (((1, 0),), ((2, 0), (0, 1)))

VMEM = pl.BlockSpec(memory_space=pltpu.VMEM)
SMEM = pl.BlockSpec(memory_space=pltpu.SMEM)
HBM = pl.BlockSpec(memory_space=pltpu.HBM)


def cost(flops, moved):
    return pl.CostEstimate(flops=flops, bytes_accessed=moved, transcendentals=0)


def parts(value, size):
    if size & (size - 1):
        return lax.div(value, size), lax.rem(value, size)
    return value >> (size.bit_length() - 1), value & (size - 1)


def brick_place(brick, across):
    rest, along_z = parts(jnp.maximum(brick, 0), across)
    return parts(rest, across)[1], along_z


def window_of(brick, grid):
    across = grid // HB
    along_y, along_z = brick_place(brick, across)
    low_y = along_y * HB - 1
    low_z = along_z * HB - 1
    start_y = jnp.clip(low_y, 0, grid - EDGE)
    start_z = jnp.clip(((low_z + 8) & -8) - 8, 0, grid - WIN)
    return start_y, low_y - start_y, start_z, low_z - start_z, along_y == across - 1


def spread(values, group_of, blank):
    row = jnp.full(group_of.shape, blank, jnp.int32)
    for entry, value in enumerate(values):
        row = jnp.where(group_of == entry, value, row)
    return row


def slot_targets(bricks, owners, capacity, group_of):
    owners = [jnp.where(brick >= 0, owner, -1) for brick, owner in zip(bricks, owners)]
    owner_row = spread(owners, group_of, -1)
    rank = jnp.zeros_like(owner_row)
    for entry, owner in enumerate(owners):
        rank += jnp.where((group_of > entry) & (owner_row == owner), 1, 0)
    return jnp.where(owner_row >= 0, owner_row * capacity + rank, -1)


def cut_windows(
    bricks, owners, latents_ref, plane, count, win, sem, pick, out_ref, base, sent_ref, line_sem
):
    grid = latents_ref.shape[1]
    channels = latents_ref.shape[3]
    listed = len(bricks)
    group, _, capacity, _ = out_ref.shape
    slots = group * capacity
    places = [window_of(brick, grid) for brick in bricks]
    copies = []
    for entry, (start_y, _, start_z, _, _) in enumerate(places):
        copy = pltpu.make_async_copy(
            latents_ref.at[
                pl.ds(plane, count),
                pl.ds(start_y, EDGE),
                pl.ds(pl.multiple_of(start_z, 8), WIN),
                :,
            ],
            win.at[entry],
            sem.at[entry],
        )
        copy.start()
        copies.append(copy)
    column = lax.broadcasted_iota(jnp.int32, (1, listed * WIN), 1)
    group_of, cell = parts(column, WIN)
    target = slot_targets(bricks, owners, capacity, group_of)

    def finish():
        shape = (EDGE * slots, listed * WIN)
        shift = spread([place[3] for place in places], group_of, FAR)
        late = spread([jnp.where(place[4], FAR, place[3]) for place in places], group_of, FAR)
        step, at = parts(lax.broadcasted_iota(jnp.int32, shape, 0), slots)
        same = at == target
        pick[0] = jnp.where(same & (step == cell - shift), 1.0, 0.0).astype(jnp.bfloat16)
        pick[1] = jnp.where(same & (step == cell - late), 1.0, 0.0).astype(jnp.bfloat16)
        for copy in copies:
            copy.wait()

        def leave(y):
            some = pl.ds(base + y * count * EDGE, count * EDGE)
            return pltpu.make_async_copy(out_ref.at[:, some], sent_ref.at[:, some], line_sem.at[y])

        def line(y, carry):
            rows = [jnp.clip(y + place[1], 0, EDGE - 1) for place in places]
            planes = [
                jnp.concatenate([win[entry, x, rows[entry]] for entry in range(listed)], axis=0)
                for x in range(count)
            ]
            cut = jnp.dot(
                pick[int(y >= EDGE - 2)],
                jnp.concatenate(planes, axis=1),
                preferred_element_type=jnp.float32,
            ).astype(jnp.bfloat16)
            for x in range(count):
                for z in range(EDGE):
                    out_ref[:, base + (y * count + x) * EDGE + z] = cut[
                        z * slots : (z + 1) * slots, x * channels : (x + 1) * channels
                    ].reshape(group, capacity, channels)
            leave(y).start()
            return carry

        for y in range(EDGE):
            line(y, 0)
        for y in range(EDGE):
            leave(y).wait()

    return target, cell, finish


def gather_own(latents, brick_ids, brick_owner, neighbor_live, group, capacity):
    grid = latents.shape[1]
    channels = latents.shape[3]
    across = grid // HB
    listed = brick_ids.shape[0]
    slots = group * capacity
    cells = HB * EDGE * EDGE

    def kernel(ids_ref, owner_ref, near_ref, latents_ref, sent_ref, out_ref, flags, win, pick, sem,
               line_sem):
        me = lax.axis_index("grp")
        bricks = [ids_ref[entry] for entry in range(listed)]
        owners = [owner_ref[entry] for entry in range(listed)]
        target, cell, finish = cut_windows(
            bricks, owners, latents_ref, 0, HB, win, sem, pick, out_ref, 0, sent_ref, line_sem
        )
        offset = lax.broadcasted_iota(jnp.int32, (1, 27), 1)
        step_x = offset // 9 - 1
        step_y = offset // 3 % 3 - 1
        step_z = offset % 3 - 1
        inside_x = (me + step_x >= 0) & (me + step_x < group)
        flags[...] = jnp.zeros_like(flags)
        for entry in range(listed):
            along_y, along_z = brick_place(bricks[entry], across)
            near_y = along_y + step_y
            near_z = along_z + step_z
            inside = inside_x & (near_y >= 0) & (near_y < across)
            inside = inside & (near_z >= 0) & (near_z < across)
            chosen = (near_ref[entry : entry + 1, :] > 0) | (offset == 13)
            flags[entry * WIN : entry * WIN + 1, 0:27] = jnp.where(inside & chosen, 1.0, 0.0)
        at = lax.broadcasted_iota(jnp.int32, (slots, listed * WIN), 0)
        chosen = jnp.where((at == target) & (cell == 0), 1.0, 0.0).astype(jnp.bfloat16)
        slot_flags = jnp.dot(
            chosen, flags[...].astype(jnp.bfloat16), preferred_element_type=jnp.float32
        )
        out_ref[:, cells] = slot_flags.astype(jnp.bfloat16).reshape(group, capacity, channels)
        last = pltpu.make_async_copy(
            out_ref.at[:, pl.ds(cells, 1)], sent_ref.at[:, pl.ds(cells, 1)], line_sem.at[EDGE]
        )
        last.start()
        finish()
        last.wait()

    return pl.pallas_call(
        kernel,
        in_specs=[SMEM, SMEM, VMEM, HBM],
        out_specs=HBM,
        out_shape=jax.ShapeDtypeStruct((group, cells + 1, capacity, channels), jnp.bfloat16),
        scratch_shapes=[
            pltpu.VMEM((group, cells + 1, capacity, channels), jnp.bfloat16),
            pltpu.VMEM((listed * WIN, channels), jnp.float32),
            pltpu.VMEM((listed, HB, EDGE, WIN, channels), jnp.bfloat16),
            pltpu.VMEM((2, EDGE * slots, listed * WIN), jnp.bfloat16),
            pltpu.SemaphoreType.DMA((listed,)),
            pltpu.SemaphoreType.DMA((EDGE + 1,)),
        ],
        compiler_params=pltpu.CompilerParams(vmem_limit_bytes=BIG),
        cost_estimate=cost(1_000_000_000, 3_000_000),
    )(brick_ids, brick_owner, neighbor_live, latents)


def gather_rims(latents, heard, listed, group, capacity):
    channels = latents.shape[3]
    slots = group * capacity
    plane_cells = EDGE * EDGE

    def kernel(heard_ref, latents_ref, sent_ref, out_ref, win_b, win_a, pick_b, pick_a, sem,
               line_sem):
        me = lax.axis_index("grp")

        def lists_of(device, near):
            both = [heard_ref[device, 0, entry] for entry in range(listed)]
            used = [near & (code >= 0) for code in both]
            halves = [parts(jnp.maximum(code, 0), HALF) for code in both]
            bricks = [jnp.where(use, half[0], -1) for use, half in zip(used, halves)]
            return bricks, [half[1] for half in halves]

        before = lists_of(jnp.where(me > 0, me - 1, group - 1), me > 0)
        after = lists_of(jnp.where(me < group - 1, me + 1, 0), me < group - 1)
        finish_b = cut_windows(
            *before, latents_ref, 0, 2, win_b, sem.at[0], pick_b, out_ref, 0, sent_ref,
            line_sem.at[0],
        )[2]
        finish_a = cut_windows(
            *after, latents_ref, HB - 1, 1, win_a, sem.at[1], pick_a, out_ref, 2 * plane_cells,
            sent_ref, line_sem.at[1],
        )[2]
        finish_b()
        finish_a()

    return pl.pallas_call(
        kernel,
        in_specs=[SMEM, HBM],
        out_specs=HBM,
        out_shape=jax.ShapeDtypeStruct(
            (group, 3 * plane_cells, capacity, channels), jnp.bfloat16
        ),
        scratch_shapes=[
            pltpu.VMEM((group, 3 * plane_cells, capacity, channels), jnp.bfloat16),
            pltpu.VMEM((listed, 2, EDGE, WIN, channels), jnp.bfloat16),
            pltpu.VMEM((listed, 1, EDGE, WIN, channels), jnp.bfloat16),
            pltpu.VMEM((2, EDGE * slots, listed * WIN), jnp.bfloat16),
            pltpu.VMEM((2, EDGE * slots, listed * WIN), jnp.bfloat16),
            pltpu.SemaphoreType.DMA((2, listed)),
            pltpu.SemaphoreType.DMA((2, EDGE)),
        ],
        compiler_params=pltpu.CompilerParams(vmem_limit_bytes=BIG),
        cost_estimate=cost(1_000_000_000, 3_000_000),
    )(heard, latents)


def weight_moves(parts_of, packed, sem, inward):
    moves = []
    start = 0
    for i, part in enumerate(parts_of):
        rows = packed.at[pl.ds(start, part.shape[0])]
        source, target = (rows, part) if inward else (part, rows)
        moves.append(pltpu.make_async_copy(source, target, sem.at[i]))
        start += part.shape[0]
    return moves


def pair_weights(up_weight, first_weight, second_weight, after):
    c1, c2 = up_weight.shape[3:]
    quad = 4 * c2
    lookup = {(parity, shift): tap for parity in (0, 1) for tap, shift in taps[parity]}

    def kernel(up_ref, first_ref, second_ref, after_ref, packed, up_out, first_out, second_out,
               sem):
        moves = weight_moves((up_out, first_out, second_out), packed, sem, False)
        for kx in range(3):
            for dy in (0, 1):
                for dz in (0, 1):
                    for py in (0, 1):
                        both = []
                        for pz in (0, 1):
                            ty = lookup.get((py, dy))
                            tz = lookup.get((pz, dz))
                            both.append(
                                jnp.zeros((c2, c1), jnp.bfloat16)
                                if ty is None or tz is None
                                else up_ref[kx, ty, tz]
                            )
                        at = (dy * 2 + dz) * c1
                        up_out[kx * 4 * c1 + at : kx * 4 * c1 + at + c1, py * 2 * c2 : (py + 1) * 2 * c2] = (
                            jnp.concatenate(both, axis=0).T
                        )
        moves[0].start()
        for raw, out, move in (
            (first_ref, first_out, moves[1]),
            (second_ref, second_out, moves[2]),
        ):
            def tile(kx, carry, raw=raw, out=out):
                for dy in (0, 1):
                    for dz in (0, 1):
                        for iy in (0, 1):
                            for iz in (0, 1):
                                for oy in (0, 1):
                                    both = []
                                    for oz in (0, 1):
                                        ky = 2 * dy + iy - oy
                                        kz = 2 * dz + iz - oz
                                        both.append(
                                            raw[kx, ky, kz]
                                            if 0 <= ky <= 2 and 0 <= kz <= 2
                                            else jnp.zeros((c2, c2), jnp.bfloat16)
                                        )
                                    at = (dy * 2 + dz) * quad + (iy * 2 + iz) * c2
                                    at = pl.multiple_of(kx * 4 * quad + at, c2)
                                    out[pl.ds(at, c2), oy * 2 * c2 : (oy + 1) * 2 * c2] = (
                                        jnp.concatenate(both, axis=1)
                                    )
                return carry

            lax.fori_loop(0, 3, tile, 0)
            move.start()
        for move in moves:
            move.wait()

    shapes = ((12 * c1, quad), (12 * quad, quad), (12 * quad, quad))
    assert sum(shape[0] for shape in shapes) <= WEIGHT_ROWS
    return pl.pallas_call(
        kernel,
        in_specs=[VMEM, VMEM, VMEM, HBM],
        out_specs=HBM,
        out_shape=jax.ShapeDtypeStruct((WEIGHT_ROWS, quad), jnp.bfloat16),
        scratch_shapes=[pltpu.VMEM(shape, jnp.bfloat16) for shape in shapes]
        + [pltpu.SemaphoreType.DMA((3,))],
        compiler_params=pltpu.CompilerParams(vmem_limit_bytes=BIG),
        cost_estimate=cost(1_000_000_000, 6_000_000),
    )(jnp.swapaxes(up_weight, 3, 4), first_weight, second_weight, after)


def pair_class(p):
    return 0 if p == 0 else 2 if p == EP - 1 else 1


def cell_class(h):
    return 0 if h == 0 else 2 if h == HEDGE - 1 else 1


class Decoder:
    def __init__(self, slots, c1, quad, limits):
        self.slots, self.c1, self.quad, self.limits = slots, c1, quad, limits

    def scratch(self):
        slots, quad = self.slots, self.quad
        return [
            pltpu.VMEM((EDGE, EDGE, EDGE, slots, self.c1), jnp.bfloat16),
            pltpu.VMEM((EEDGE, EP, EP, slots, quad), jnp.bfloat16),
            pltpu.VMEM((HEDGE, HP, HP, slots, quad), jnp.bfloat16),
            pltpu.VMEM((3, EP, EP, slots, quad // 2), jnp.bfloat16),
            pltpu.VMEM((3, HP, HP, slots, quad), jnp.bfloat16),
            pltpu.VMEM((slots, self.c1), jnp.float32),
            pltpu.VMEM((12 * self.c1, quad), jnp.bfloat16),
            pltpu.VMEM((12 * quad, quad), jnp.bfloat16),
            pltpu.VMEM((12 * quad, quad), jnp.bfloat16),
            pltpu.SemaphoreType.DMA((3,)),
        ]

    def masks(self, flags, emask, hmask, classes):
        half, c2 = self.quad // 2, self.quad // 4
        wide = {
            cx * 9 + n: jnp.broadcast_to(flags[:, cx * 9 + n : cx * 9 + n + 1], (self.slots, half))
            for cx in classes
            for n in range(9)
        }
        left = lax.broadcasted_iota(jnp.int32, (self.slots, half), 1) < c2
        for cx in classes:
            for py in range(EP):
                for pz in range(EP):
                    n = cx * 9 + pair_class(py) * 3 + pair_class(pz)
                    emask[cx, py, pz] = wide[n].astype(jnp.bfloat16)
            mixed = {}
            for py in range(HP):
                for pz in range(HP):
                    for ty in (0, 1):
                        n = cx * 9 + cell_class(2 * py + ty) * 3
                        key = (n + cell_class(2 * pz), n + cell_class(2 * pz + 1))
                        if key not in mixed:
                            mixed[key] = jnp.where(left, wide[key[0]], wide[key[1]]).astype(
                                jnp.bfloat16
                            )
                        hmask[cx, py, pz, :, ty * half : (ty + 1) * half] = mixed[key]

    def raise_cells(self, reg, up_ref, emask, ext, edges):
        depth = 4 * self.c1
        for parity, shifts in ((0, ((1, 0),)), (1, ((2, 0), (0, 1)))):
            planes = [edge for edge in edges if edge % 2 == parity]
            weight = jnp.concatenate(
                [up_ref[tap * depth : (tap + 1) * depth] for tap, _ in shifts], axis=0
            )
            for blocks in self.chunks(planes, EP, 0):
                pieces = [
                    jnp.concatenate(
                        [reg[x // 2 + shift, y + dy, z + dz] for x, y, z in blocks], axis=0
                    )
                    for _, shift in shifts
                    for dy in (0, 1)
                    for dz in (0, 1)
                ]
                value = jnp.dot(
                    jnp.concatenate(pieces, axis=1), weight, preferred_element_type=jnp.float32
                ).astype(jnp.bfloat16)
                for i, (x, y, z) in enumerate(blocks):
                    mask = emask[pair_class(x // 2), y, z]
                    mask = jnp.concatenate([mask, mask], axis=1)
                    ext[x, y, z] = value[i * self.slots : (i + 1) * self.slots] * mask

    def conv(self, source, blocks, weight_ref):
        pieces = [
            jnp.concatenate([source[x + kx, y + dy, z + dz] for x, y, z in blocks], axis=0)
            for kx in range(3)
            for dy in (0, 1)
            for dz in (0, 1)
        ]
        return jnp.dot(
            jnp.concatenate(pieces, axis=1), weight_ref[...], preferred_element_type=jnp.float32
        )

    def chunks(self, planes, pairs, step):
        blocks = [(x, y, z) for x in planes for y in range(pairs) for z in range(pairs)]
        count = -(-len(blocks) * self.slots // self.limits[step])
        ends = [len(blocks) * i // count for i in range(count + 1)]
        return [blocks[start:end] for start, end in zip(ends, ends[1:])]

    def hide(self, ext, first_ref, hmask, hid, planes):
        for blocks in self.chunks(planes, HP, 1):
            value = self.conv(ext, blocks, first_ref)
            value = (value * (1.0 / (1.0 + jnp.exp(-value)))).astype(jnp.bfloat16)
            for i, (x, y, z) in enumerate(blocks):
                one = value[i * self.slots : (i + 1) * self.slots]
                hid[x, y, z] = one * hmask[cell_class(x), y, z]

    def refine(self, ext, hid, second_ref, rows, planes):
        half = self.quad // 2
        for blocks in self.chunks(planes, OP, 2):
            value = self.conv(hid, blocks, second_ref)
            for i, (x, y, z) in enumerate(blocks):
                one = value[i * self.slots : (i + 1) * self.slots]
                one = one + ext[x + 2, y + 1, z + 1].astype(jnp.float32)
                one = one.astype(jnp.bfloat16)
                for ty in (0, 1):
                    line = (planes.index(x) * BE + 2 * y + ty) * OP + z
                    rows[:, line * half : (line + 1) * half] = one[:, ty * half : (ty + 1) * half]


INNER_E, INNER_H, INNER_O = (2, 9), (2, 7), (2, 5)
KEPT_E = (2, 3, 7, 8)
KEPT_H = (2, 3, 5, 6)
KEPT_ROWS = 64


def decode_inner(own, pairs):
    group, _, capacity, c1 = own.shape
    quad = pairs.shape[1]
    slots = group * capacity
    plane = BE * BE * quad // 4
    steps = Decoder(slots, c1, quad, INNER_ROWS)
    width = (INNER_O[1] - INNER_O[0]) * plane

    def kernel(own_ref, packed, out_ref, kept,
               reg, ext, hid, emask, hmask, flags, up_ref, first_ref, second_ref, wsem, rows, sem):
        weights = weight_moves((up_ref, first_ref, second_ref), packed, wsem, True)
        for move in weights:
            move.start()
        flags[...] = own_ref[:, HB * EDGE * EDGE].reshape(slots, c1).astype(jnp.float32)

        def load(y, carry):
            for x in range(HB):
                for z in range(EDGE):
                    reg[1 + x, y, z] = own_ref[:, (y * HB + x) * EDGE + z].reshape(slots, c1)
            return carry

        lax.fori_loop(0, EDGE, load, 0, unroll=True)
        steps.masks(flags, emask, hmask, (1,))
        weights[0].wait()

        steps.raise_cells(reg, up_ref, emask, ext, list(range(*INNER_E)))
        copies = [
            pltpu.make_async_copy(ext.at[e], kept.at[i], sem.at[i])
            for i, e in enumerate(KEPT_E)
        ]
        for copy in copies:
            copy.start()

        weights[1].wait()

        steps.hide(ext, first_ref, hmask, hid, list(range(*INNER_H)))
        more = [
            pltpu.make_async_copy(
                hid.at[h], kept.at[4 + i, pl.ds(0, HP), pl.ds(0, HP)], sem.at[4 + i]
            )
            for i, h in enumerate(KEPT_H)
        ]
        for copy in more:
            copy.start()

        weights[2].wait()

        steps.refine(ext, hid, second_ref, rows, list(range(*INNER_O)))
        last = pltpu.make_async_copy(
            rows, out_ref.at[:, pl.ds(INNER_O[0] * plane, width)], sem.at[8]
        )
        last.start()
        for copy in copies + more + [last]:
            copy.wait()

    return pl.pallas_call(
        kernel,
        in_specs=[VMEM, HBM],
        out_specs=[HBM] * 2,
        out_shape=[
            jax.ShapeDtypeStruct((slots, BE * plane), jnp.bfloat16),
            jax.ShapeDtypeStruct((KEPT_ROWS, EP, EP, slots, quad), jnp.bfloat16),
        ],
        scratch_shapes=steps.scratch()
        + [pltpu.VMEM((slots, width), jnp.bfloat16), pltpu.SemaphoreType.DMA((9,))],
        compiler_params=pltpu.CompilerParams(vmem_limit_bytes=50_000_000),
        cost_estimate=cost(8_000_000_000, 6_000_000),
    )(own, pairs)


def decode_outer(own, rims, out, kept, pairs):
    group, _, capacity, c1 = own.shape
    quad = pairs.shape[1]
    slots = group * capacity
    plane = BE * BE * quad // 4
    steps = Decoder(slots, c1, quad, OUTER_ROWS)
    plane_cells = EDGE * EDGE
    low_o = INNER_O[0]
    high_o = BE - INNER_O[1]

    def kernel(own_ref, rims_ref, packed, kept, out_in, out_ref,
               reg, ext, hid, emask, hmask, flags, up_ref, first_ref, second_ref, wsem, rows, sem):
        weights = weight_moves((up_ref, first_ref, second_ref), packed, wsem, True)
        for move in weights:
            move.start()
        copies = [
            pltpu.make_async_copy(kept.at[i], ext.at[e], sem.at[i])
            for i, e in enumerate(KEPT_E)
        ] + [
            pltpu.make_async_copy(
                kept.at[4 + i, pl.ds(0, HP), pl.ds(0, HP)], hid.at[h], sem.at[4 + i]
            )
            for i, h in enumerate(KEPT_H)
        ]
        for copy in copies:
            copy.start()
        flags[...] = own_ref[:, HB * plane_cells].reshape(slots, c1).astype(jnp.float32)

        def turned(row, shift):
            value = rims_ref[:, row].reshape(slots, c1)
            cut = (shift % group) * capacity
            return jnp.concatenate([value[cut:], value[:cut]], axis=0)

        def load(y, carry):
            for z in range(EDGE):
                at = y * EDGE + z
                reg[0, y, z] = turned(2 * plane_cells + at, -1)
                reg[1, y, z] = own_ref[:, y * HB * EDGE + z].reshape(slots, c1)
                reg[HB, y, z] = own_ref[:, (y * HB + HB - 1) * EDGE + z].reshape(slots, c1)
                reg[HB + 1, y, z] = turned(2 * y * EDGE + z, 1)
                reg[HB + 2, y, z] = turned((2 * y + 1) * EDGE + z, 1)
            return carry

        lax.fori_loop(0, EDGE, load, 0, unroll=True)
        steps.masks(flags, emask, hmask, (0, 1, 2))
        weights[0].wait()

        steps.raise_cells(
            reg, up_ref, emask, ext, list(range(INNER_E[0])) + list(range(INNER_E[1], EEDGE))
        )
        for copy in copies:
            copy.wait()

        weights[1].wait()

        steps.hide(
            ext, first_ref, hmask, hid,
            list(range(INNER_H[0])) + list(range(INNER_H[1], HEDGE)),
        )
        weights[2].wait()

        steps.refine(
            ext, hid, second_ref, rows, list(range(low_o)) + list(range(INNER_O[1], BE))
        )
        ends = [
            pltpu.make_async_copy(
                rows.at[:, pl.ds(0, low_o * plane)], out_ref.at[:, pl.ds(0, low_o * plane)],
                sem.at[8],
            ),
            pltpu.make_async_copy(
                rows.at[:, pl.ds(low_o * plane, high_o * plane)],
                out_ref.at[:, pl.ds(INNER_O[1] * plane, high_o * plane)],
                sem.at[9],
            ),
        ]
        for copy in ends:
            copy.start()
        for copy in ends:
            copy.wait()

    return pl.pallas_call(
        kernel,
        in_specs=[VMEM] * 2 + [HBM] * 3,
        out_specs=HBM,
        out_shape=jax.ShapeDtypeStruct((slots, BE * plane), jnp.bfloat16),
        scratch_shapes=steps.scratch()
        + [
            pltpu.VMEM((slots, (low_o + high_o) * plane), jnp.bfloat16),
            pltpu.SemaphoreType.DMA((10,)),
        ],
        input_output_aliases={4: 0},
        compiler_params=pltpu.CompilerParams(vmem_limit_bytes=50_000_000),
        cost_estimate=cost(8_000_000_000, 6_000_000),
    )(own, rims, pairs, kept, out)


def to_owners(array):
    return lax.all_to_all(array, "grp", split_axis=0, concat_axis=0, tiled=True)


def local(latents, up_weight, first_weight, second_weight, brick_ids, brick_owner, neighbor_live):
    group = lax.axis_size("grp")
    listed = brick_ids.shape[0]
    capacity = max(2, listed // group)
    assert latents.shape[0] == HB
    both = jnp.where(brick_ids >= 0, brick_ids * HALF + brick_owner, -1)
    heard = to_owners(jnp.broadcast_to(both, (group, 1, listed)))
    own = gather_own(latents, brick_ids, brick_owner, neighbor_live, group, capacity)
    own = to_owners(own)
    rims = gather_rims(latents, heard, listed, group, capacity)
    rims = to_owners(rims)
    pairs = pair_weights(up_weight, first_weight, second_weight, heard)
    out, kept = decode_inner(own, pairs)
    return decode_outer(own, rims, out, kept, pairs)


def solution(mesh):
    in_specs = (
        P(("shape", "grp"), None, None, None),
        P(),
        P(),
        P(),
        P(("shape", "grp")),
        P(("shape", "grp")),
        P(("shape", "grp"), None),
    )
    out_specs = P(("shape", "grp"), None)
    return jax.shard_map(local, mesh=mesh, in_specs=in_specs, out_specs=out_specs, check_vma=False)
```
